128 devices in a mesh: blk: 64 (over z, y_hi, x, core), space: 2 (over y_lo).
Axes of the slice: x: 4, y: 4 (y_hi: 2, y_lo: 2; y = y_hi * 2 + y_lo), z: 4, core: 2. Of those that a mesh axis runs over, the one named last changes fastest.
Arguments:
- distribution: bfloat16 [2, 1792, 32, 2048], P(None, 'blk', 'space'), may hold values from -6 to 6
- face_signs: int32 [1792, 32], P('blk', 'space'), may hold values from 0 to 1
- stream_speed: float32 [2048], replicated, may hold values from 0.5 to 2
- factors: bfloat16 [3, 2048, 2048], P(None, 'blk'), may hold values from -0.125 to 0.125
- pair_list: int32 [3, 2], replicated, may hold values from 0 to 1
- frequency: float32 [3], replicated, may hold values from 0.5 to 2
Outputs:
- advanced: bfloat16 [2, 1792, 32, 2048], P(None, 'blk', 'space')
- collision: bfloat16 [3, 1792, 32, 2048], P(None, 'blk', 'space')
The draws below stay inside these ranges and needn't reach their ends.
Inputs may be any that keep to these rules, and one draw needn't show every extreme that they name: Pair p gives the collision term of species pair_list[p, 0] against species pair_list[p, 1]. `face_signs`: 1 where the flow at a cell's face toward higher x goes toward higher x, 0 where it goes toward lower x; the face after the grid's last cell is a wall and its entry is not read.
All inputs are finite; a program needn't handle non-finite values.
Results may differ from the reference program's by a relative error of at most 0.0064.
Values may be sent and summed in bfloat16 or wider, within the bound.
No kernel may reach another device: no remote copies, remote signals or barrier semaphores. Data moves between devices by JAX's collectives and lax.ppermute only.
A program may use at most 192 MiB of HBM per device.

```python
import math
import jax
import jax.numpy as jnp
from jax import lax

K = 2048
S = 2
P_SIZE = 3
LINES_DEV = 28
RANK = 2048
LINES = 1792
NX = 32
N_BLK = 64


def touch_ends(values, own_key, low, largest):
    spot = [jax.random.randint(jax.random.fold_in(own_key, axis), (), 0, length) for axis, length in enumerate(values.shape)]
    widest = values.shape.index(max(values.shape))
    next_to = spot[:widest] + [(spot[widest] + 1) % values.shape[widest]] + spot[widest + 1:]
    return values.at[tuple(spot)].set(low).at[tuple(next_to)].set(largest)


def block_levels(key, shape, pieces, low, high):
    def one(dim, parts):
        heights = jax.random.uniform(jax.random.fold_in(jax.random.fold_in(key, 6), dim), (parts,), jnp.float32, low / len(pieces), high / len(pieces))
        return jnp.repeat(jnp.exp(heights), shape[dim] // parts).reshape((-1,) + (1,) * (len(shape) - dim - 1))

    factor_of = one(*pieces[0])
    for cut in pieces[1:]:
        factor_of = factor_of * one(*cut)
    return factor_of


def scatter_about(key, dims, deviation, bound, cuts=(), kind=jnp.bfloat16):
    loudness = block_levels(key, dims, cuts, -0.22, 0.18) if cuts else 1.0
    drawn = jax.random.normal(key, dims, jnp.float32) * deviation * loudness
    return jnp.minimum(jnp.maximum(drawn, -bound), bound).astype(kind)


def setup_inputs(seed: int = 0) -> dict:
    key_list = jax.random.split(jax.random.key(seed), 7)
    return {
        "distribution": scatter_about(key_list[0], (S, LINES, NX, K), 1.0, 6.0, ((1, 64), (2, 2))),
        "face_signs": touch_ends(jax.random.randint(key_list[1], (LINES, NX), 0, 2), jax.random.fold_in(key_list[1], 1), 0, 1).astype(jnp.int32),
        "stream_speed": jnp.clip(jnp.exp(jax.random.uniform(key_list[2], (K,), jnp.float32, math.log(0.5), math.log(2.0))), 0.5, 2.0),
        "factors": scatter_about(key_list[3], (3, RANK, K), K ** -0.5, 0.125, ((1, 64),)),
        "pair_list": touch_ends(jax.random.randint(key_list[4], (P_SIZE, 2), 0, S), jax.random.fold_in(key_list[4], 1), 0, S - 1).astype(jnp.int32),
        "frequency": jnp.clip(jnp.exp(jax.random.uniform(key_list[5], (P_SIZE,), jnp.float32, math.log(0.5), math.log(2.0))), 0.5, 2.0),
    }


courant = 0.3


def transport(distribution, face_dir, stream_speed, extent):
    field = jnp.pad(distribution.astype(jnp.float32), ((0, 0), (0, 0), (2, 2), (0, 0)))
    upper = field[:, :, 1:extent + 2] + 0.5 * (field[:, :, 1:extent + 2] - field[:, :, 0:extent + 1])
    lower = field[:, :, 2:extent + 3] - 0.5 * (field[:, :, 3:extent + 4] - field[:, :, 2:extent + 3])
    direction = face_dir[None, :, :, None]
    state = jnp.where(direction > 0, upper, lower)
    flux_face = direction * stream_speed * state
    return (field[:, :, 2:extent + 2] - courant * (flux_face[:, :, 1:] - flux_face[:, :, :-1])).astype(jnp.bfloat16)


def reference(distribution, face_signs, stream_speed, factors, pair_list, frequency):
    sign_vals = (2 * face_signs - 1).astype(jnp.float32)
    zero_col = jnp.zeros((LINES, 1), jnp.float32)
    face_dir = jnp.concatenate([zero_col, sign_vals[:, :NX - 1], zero_col], axis=1)
    advanced = transport(distribution, face_dir, stream_speed, NX)
    row_count = LINES_DEV * NX
    blocks = jnp.moveaxis(advanced.reshape(S, N_BLK, row_count, K), 1, 0)

    def collide(block_rows):
        left_tf = jnp.stack([lax.dot_general(block_rows[s_idx], factors[0], (((1,), (1,)), ((), ())), preferred_element_type=jnp.float32) for s_idx in range(S)])
        right_tf = jnp.stack([lax.dot_general(block_rows[s_idx], factors[1], (((1,), (1,)), ((), ())), preferred_element_type=jnp.float32) for s_idx in range(S)])
        outputs = []
        for pair_idx in range(P_SIZE):
            product = (frequency[pair_idx] * left_tf[pair_list[pair_idx, 0]] * right_tf[pair_list[pair_idx, 1]]).astype(jnp.bfloat16)
            outputs.append(jnp.dot(product, factors[2], preferred_element_type=jnp.float32).astype(jnp.bfloat16))
        return jnp.stack(outputs)

    results = lax.map(collide, blocks)
    collision = jnp.moveaxis(results, 0, 1).reshape(P_SIZE, LINES, NX, K)
    return advanced, collision
```

```python
import functools
import jax
import jax.numpy as jnp
from jax import lax
from jax.experimental import pallas as pl
from jax.experimental.pallas import tpu as pltpu
from jax.sharding import PartitionSpec as P

courant = 0.3
AXES = ("blk", "space")
SIZES = (4, 4, 4, 2)


def flat_index(z, y, x, core):
    return (((z * 2 + y // 2) * 4 + x) * 2 + core) * 2 + y % 2


def pairs_of(move):
    pairs = []
    for z in range(4):
        for y in range(4):
            for x in range(4):
                for core in range(2):
                    target = [v % n for v, n in zip(move(z, y, x, core), SIZES)]
                    pairs.append((flat_index(z, y, x, core), flat_index(*target)))
    return pairs


def along(step, first):
    return pairs_of(
        lambda z, y, x, core: (z, y, x + step, core)
        if (core == 0) == first
        else (z + step, y, x, core)
    )


PARTNER = pairs_of(lambda z, y, x, core: (z, y, x, 1 - core))
CROSS = pairs_of(lambda z, y, x, core: (z, 3 - y, x, core))
SIDE = pairs_of(lambda z, y, x, core: (z, y ^ 1, x, core))
UP1, DOWN1, FAR1 = along(1, True), along(-1, True), along(2, True)
UP2, DOWN2 = along(1, False), along(-1, False)


def send(array, pairs):
    return lax.ppermute(array, AXES, pairs)


def transport_kernel(where_ref, speed_ref, dirs_ref, halo_ref, cells_ref, out_ref):
    first_part = where_ref[0] == 0
    species, lines, cells, coeffs = cells_ref.shape
    speed = speed_ref[...]
    row = lax.broadcasted_iota(jnp.int32, (cells, coeffs), 0)

    def one(index, carry):
        s, l = index // lines, index % lines
        f = cells_ref[s, l].astype(jnp.float32)
        halo = halo_ref[s, l].astype(jnp.float32)
        h0, h1 = halo[0:1], halo[1:2]
        zero = jnp.zeros_like(h0)
        left2, left1 = jnp.where(first_part, zero, h0), jnp.where(first_part, zero, h1)
        right1, right2 = jnp.where(first_part, h0, zero), jnp.where(first_part, h1, zero)
        d_right = jnp.tile(dirs_ref[l, 0:cells], (1, coeffs // 128))
        d_first = jnp.tile(dirs_ref[l, cells : cells + 1], (1, coeffs // 128))
        before = jnp.where(row == 0, left1, pltpu.roll(f, 1, 0))
        after = jnp.where(row == cells - 1, right1, pltpu.roll(f, cells - 1, 0))
        upper = f + 0.5 * (f - before)
        lower = f - 0.5 * (after - f)
        lower_last = right1 - 0.5 * (right2 - right1)
        lower_next = jnp.where(row == cells - 1, lower_last, pltpu.roll(lower, cells - 1, 0))
        flux = d_right * speed * jnp.where(d_right > 0, upper, lower_next)
        upper_first = left1 + 0.5 * (left1 - left2)
        flux_first = d_first * speed * jnp.where(d_first > 0, upper_first, lower[0:1])
        flux_before = jnp.where(row == 0, flux_first, pltpu.roll(flux, 1, 0))
        out_ref[s, l] = (f - courant * (flux - flux_before)).astype(jnp.bfloat16)
        return carry

    lax.fori_loop(0, species * lines, one, 0)


def transport(cells, halo, dirs, speed, where):
    species, lines, count, coeffs = cells.shape
    step = 4
    return pl.pallas_call(
        transport_kernel,
        grid=(lines // step,),
        in_specs=[
            pl.BlockSpec(memory_space=pltpu.SMEM),
            pl.BlockSpec((1, coeffs), lambda i: (0, 0)),
            pl.BlockSpec((step, dirs.shape[1], 128), lambda i: (i, 0, 0)),
            pl.BlockSpec((species, step, 2, coeffs), lambda i: (0, i, 0, 0)),
            pl.BlockSpec((species, step, count, coeffs), lambda i: (0, i, 0, 0)),
        ],
        out_specs=pl.BlockSpec((species, step, count, coeffs), lambda i: (0, i, 0, 0)),
        out_shape=jax.ShapeDtypeStruct(cells.shape, jnp.bfloat16),
        cost_estimate=pl.CostEstimate(
            flops=30 * cells.size, bytes_accessed=4 * cells.size, transcendentals=0
        ),
        name="transport",
    )(where, speed, dirs, halo, cells)


def collide_kernel(tiles, first, last, *refs):
    freq_ref, pair_ref, adv_ref = refs[:3]
    groups = refs[3 : 3 + len(tiles_groups(tiles))]
    rest = refs[3 + len(groups) :]
    out_ref = rest[-1]
    acc_ref = None if first else rest[0]
    species, rows, coeffs = adv_ref.shape
    pair_count = out_ref.shape[0]
    block = rows // 2
    nt = (((1,), (1,)), ((), ()))

    def part(index, which):
        ref = groups[index]
        return ref[:, which].reshape(-1, coeffs)

    def step(i, carry):
        at = pl.ds(pl.multiple_of(i * block, block), block)
        a = adv_ref[:, at, :].reshape(species * block, coeffs)
        for t, tile in enumerate(tiles):
            lefts, rights = [], []
            for half in tile:
                w = jnp.concatenate([part(g, 0) for g in half] + [part(g, 1) for g in half], axis=0)
                both = lax.dot_general(a, w, nt, preferred_element_type=jnp.float32)
                n = both.shape[1] // 2
                lefts.append(both[:, :n])
                rights.append(both[:, n:])
            left = jnp.concatenate(lefts, axis=1)
            right = jnp.concatenate(rights, axis=1)
            down = jnp.concatenate([part(g, 2) for half in tile for g in half], axis=0)
            for p in range(pair_count):
                lp = jnp.where(pair_ref[p, 0] == 1, left[block:], left[:block])
                rp = jnp.where(pair_ref[p, 1] == 1, right[block:], right[:block])
                product = (freq_ref[p] * lp * rp).astype(jnp.bfloat16)
                term = jnp.dot(product, down, preferred_element_type=jnp.float32)
                if t > 0:
                    term = out_ref[p, at, :] + term
                elif not first:
                    term = acc_ref[p, at, :] + term
                out_ref[p, at, :] = term.astype(out_ref.dtype)
        return carry

    lax.fori_loop(0, 2, step, 0)


def tiles_groups(tiles):
    return [g for tile in tiles for half in tile for g in half]


def collide(adv, frequency, pair_list, tiles, acc, last):
    arrays, numbered = [], []
    for tile in tiles:
        numbered.append([])
        for half in tile:
            numbered[-1].append(list(range(len(arrays), len(arrays) + len(half))))
            arrays.extend(half)
    species, rows, coeffs = adv.shape
    pairs_count = pair_list.shape[0]
    ranks = sum(a.shape[0] * a.shape[2] for a in arrays)
    dtype = jnp.bfloat16 if last else jnp.float32
    assert not last or len(tiles) == 1
    shape = (pairs_count, rows, coeffs)
    vmem = pl.BlockSpec(memory_space=pltpu.VMEM)
    smem = pl.BlockSpec(memory_space=pltpu.SMEM)
    operands = [frequency, pair_list, adv] + arrays + ([] if acc is None else [acc])
    return pl.pallas_call(
        functools.partial(collide_kernel, numbered, acc is None, last),
        in_specs=[smem, smem] + [vmem] * (len(operands) - 2),
        out_specs=vmem,
        out_shape=jax.ShapeDtypeStruct(shape, dtype),
        input_output_aliases={} if acc is None or last else {len(operands) - 1: 0},
        cost_estimate=pl.CostEstimate(
            flops=2 * ranks * coeffs * rows * (2 * species + pairs_count),
            bytes_accessed=2 * (adv.size + 3 * ranks * coeffs),
            transcendentals=0,
        ),
        name="collide",
    )(*operands)


def gather_set(mine):
    up, down, far = send(mine, UP1), send(mine, DOWN1), send(mine, FAR1)
    group = jnp.concatenate([mine, up, down, far], axis=0)
    return group


def spread(group):
    half = group.shape[0] // 2
    up, down = send(group, UP2), send(group, DOWN2)
    up_far = send(up[:half], UP2)
    down_far = send(down[half:], DOWN2)
    return up, down, up_far, down_far


def swap(array):
    return send(array, PARTNER)


def local(distribution, face_signs, stream_speed, factors, pair_list, frequency):
    species, lines, cells, coeffs = distribution.shape
    here = lax.axis_index("space")
    mine = factors[None]
    group_o = gather_set(mine)
    cross = send(mine, CROSS)

    edge = jnp.where(here == 0, distribution[:, :, cells - 2 :], distribution[:, :, :2])
    last_sign = face_signs[:, cells - 1].astype(jnp.bfloat16)
    sign_row = jnp.pad(last_sign, (0, coeffs - lines))[None]
    sign_rows = jnp.concatenate([sign_row, jnp.zeros((7, coeffs), jnp.bfloat16)], axis=0)
    packet = jnp.concatenate([edge.reshape(-1, coeffs), sign_rows], axis=0)
    packet = send(packet, SIDE)
    halo = packet[: species * lines * 2].reshape(species, lines, 2, coeffs)
    got_sign = packet[species * lines * 2, :lines].astype(jnp.int32)
    signs = (2 * face_signs - 1).astype(jnp.float32)
    column = jnp.arange(cells, dtype=jnp.int32)[None, :]
    d_right = jnp.where((here == 1) & (column == cells - 1), 0.0, signs)
    d_first = jnp.where(here == 0, 0.0, (2 * got_sign - 1).astype(jnp.float32))
    dirs = jnp.concatenate([d_right, jnp.broadcast_to(d_first[:, None], (lines, 8))], axis=1)
    dirs = jnp.broadcast_to(dirs[:, :, None], (lines, cells + 8, 128))
    advanced = transport(
        distribution, halo, dirs, stream_speed[None], here.astype(jnp.int32)[None]
    )
    adv = advanced.reshape(species, lines * cells, coeffs)

    step = functools.partial(collide, adv, frequency, pair_list)
    up_o, down_o, upf_o, downf_o = spread(group_o)
    group_c = gather_set(cross)
    up_c, down_c, upf_c, downf_c = spread(group_c)

    acc = step([[[group_o], [swap(group_o)]]], None, False)
    acc = step([[[up_o], [swap(up_o)]], [[down_o], [swap(down_o)]]], acc, False)
    acc = step([[[upf_o, downf_o], [swap(upf_o), swap(downf_o)]]], acc, False)
    acc = step([[[group_c], [swap(group_c)]]], acc, False)
    acc = step([[[up_c], [swap(up_c)]], [[down_c], [swap(down_c)]]], acc, False)
    out = step([[[upf_c, downf_c], [swap(upf_c), swap(downf_c)]]], acc, True)
    collision = out.reshape(pair_list.shape[0], lines, cells, coeffs)
    return (advanced, collision)


def solution(mesh):
    return jax.shard_map(
        local,
        mesh=mesh,
        in_specs=(
            P(None, "blk", "space", None),
            P("blk", "space"),
            P(),
            P(None, "blk", None),
            P(),
            P(),
        ),
        out_specs=(P(None, "blk", "space", None), P(None, "blk", "space", None)),
        check_vma=False,
    )
```

```python
import functools
import jax
import jax.numpy as jnp
from jax import lax
from jax.experimental import pallas as pl
from jax.experimental.pallas import tpu as pltpu
from jax.sharding import PartitionSpec as P

courant = 0.3
AXES = ("blk", "space")
SIZES = (4, 4, 4, 2)


def flat_index(z, y, x, core):
    return (((z * 2 + y // 2) * 4 + x) * 2 + core) * 2 + y % 2


def pairs_of(move):
    pairs = []
    for z in range(4):
        for y in range(4):
            for x in range(4):
                for core in range(2):
                    target = [v % n for v, n in zip(move(z, y, x, core), SIZES)]
                    pairs.append((flat_index(z, y, x, core), flat_index(*target)))
    return pairs


def along(step, first):
    return pairs_of(
        lambda z, y, x, core: (z, y, x + step, core)
        if (core == 0) == first
        else (z + step, y, x, core)
    )


PARTNER = pairs_of(lambda z, y, x, core: (z, y, x, 1 - core))
CROSS = pairs_of(lambda z, y, x, core: (z, 3 - y, x, core))
SIDE = pairs_of(lambda z, y, x, core: (z, y ^ 1, x, core))
UP1, DOWN1, FAR1 = along(1, True), along(-1, True), along(2, True)
UP2, DOWN2 = along(1, False), along(-1, False)


def send(array, pairs):
    return lax.ppermute(array, AXES, pairs)


ANY = pl.BlockSpec(memory_space=pl.ANY)
SMEM = pl.BlockSpec(memory_space=pltpu.SMEM)
HBM = pl.BlockSpec(memory_space=pltpu.HBM)
VMEM = pl.BlockSpec(memory_space=pltpu.VMEM)
DMA = pltpu.SemaphoreType.DMA


def cost(flops, moved):
    return pl.CostEstimate(flops=flops, bytes_accessed=moved, transcendentals=0)


def packet_kernel(where_ref, signs_ref, cells_ref, out_ref, rows, sem):
    first_part = where_ref[0] == 0
    species, lines, cells, coeffs = cells_ref.shape
    start = pl.multiple_of(jnp.where(first_part, cells - 8, 0), 8)
    copy = pltpu.make_async_copy(cells_ref.at[:, :, pl.ds(start, 8), :], rows, sem)
    copy.start()
    out_ref[species * lines] = jnp.zeros((2, coeffs), jnp.bfloat16)
    last = signs_ref[cells - 1 : cells, :].astype(jnp.float32)
    last = jnp.concatenate([last, last], axis=0).astype(jnp.bfloat16)
    out_ref[species * lines, :, 0:lines] = last
    copy.wait()

    def one(l, carry):
        for s in range(species):
            eight = rows[s, l].astype(jnp.float32)
            edge = jnp.where(first_part, eight[6:8], eight[0:2])
            out_ref[s * lines + l] = edge.astype(jnp.bfloat16)
        return carry

    lax.fori_loop(0, lines, one, 0)


def packet_of(cells, signs, where):
    species, lines, count, coeffs = cells.shape
    return pl.pallas_call(
        packet_kernel,
        in_specs=[SMEM, VMEM, HBM],
        out_specs=VMEM,
        out_shape=jax.ShapeDtypeStruct((species * lines + 1, 2, coeffs), jnp.bfloat16),
        scratch_shapes=[pltpu.VMEM((species, lines, 8, coeffs), jnp.bfloat16), DMA],
        cost_estimate=cost(cells.size, cells.size),
        compiler_params=pltpu.CompilerParams(vmem_limit_bytes=8 << 20),
        name="packet",
    )(where, signs, cells)


CHUNKS = 4


def transport_kernel(where_ref, speed_ref, signs_ref, packet_ref, cells_hbm, out_ref, out_hbm, cells_ref, in_sem, out_sem):
    first_part = where_ref[0] == 0
    species, lines, cells, coeffs = cells_ref.shape
    chunk = lines // CHUNKS

    def arriving(c):
        at = pl.ds(c * chunk, chunk)
        return pltpu.make_async_copy(cells_hbm.at[:, at], cells_ref.at[:, at], in_sem.at[c])

    def leaving(c):
        at = pl.ds(c * chunk, chunk)
        return pltpu.make_async_copy(out_ref.at[:, at], out_hbm.at[:, at], out_sem.at[c])

    for c in range(CHUNKS):
        arriving(c).start()
    width = 512
    row = lax.broadcasted_iota(jnp.int32, (cells, width), 0)
    row1 = lax.broadcasted_iota(jnp.int32, (cells, lines), 0)
    lane = lax.broadcasted_iota(jnp.int32, (cells, lines), 1)
    signs = (2 * signs_ref[...] - 1).astype(jnp.float32)
    signs = jnp.where(jnp.logical_and(row1 == cells - 1, jnp.logical_not(first_part)), 0.0, signs)
    got = 2.0 * packet_ref[species * lines, 0:1, 0:lines].astype(jnp.float32) - 1.0
    got = jnp.where(first_part, 0.0, got)

    def one(l, carry):
        d_right = jnp.sum(jnp.where(lane == l, signs, 0.0), axis=1, keepdims=True)
        d_first = jnp.sum(jnp.where(lane[0:1] == l, got, 0.0), axis=1, keepdims=True)
        d_right = jnp.broadcast_to(d_right, (cells, width))
        d_first = jnp.broadcast_to(d_first, (1, width))
        for c in range(coeffs // width):
            at = slice(c * width, (c + 1) * width)
            speed = speed_ref[:, at]
            for s in range(species):
                f = cells_ref[s, l, :, at].astype(jnp.float32)
                halo = packet_ref[s * lines + l, :, at].astype(jnp.float32)
                h0, h1 = halo[0:1], halo[1:2]
                zero = jnp.zeros_like(h0)
                left2, left1 = jnp.where(first_part, zero, h0), jnp.where(first_part, zero, h1)
                right1, right2 = jnp.where(first_part, h0, zero), jnp.where(first_part, h1, zero)
                before = jnp.where(row == 0, left1, pltpu.roll(f, 1, 0))
                after = jnp.where(row == cells - 1, right1, pltpu.roll(f, cells - 1, 0))
                upper = f + 0.5 * (f - before)
                lower = f - 0.5 * (after - f)
                lower_last = right1 - 0.5 * (right2 - right1)
                lower_next = jnp.where(row == cells - 1, lower_last, pltpu.roll(lower, cells - 1, 0))
                flux = d_right * speed * jnp.where(d_right > 0, upper, lower_next)
                upper_first = left1 + 0.5 * (left1 - left2)
                flux_first = d_first * speed * jnp.where(d_first > 0, upper_first, lower[0:1])
                flux_before = jnp.where(row == 0, flux_first, pltpu.roll(flux, 1, 0))
                out_ref[s, l, :, at] = (f - courant * (flux - flux_before)).astype(jnp.bfloat16)
        return carry

    for c in range(CHUNKS):
        arriving(c).wait()
        lax.fori_loop(c * chunk, (c + 1) * chunk, one, 0)
        leaving(c).start()
    for c in range(CHUNKS):
        leaving(c).wait()


def transport(cells, packet, signs, speed, where):
    return pl.pallas_call(
        transport_kernel,
        in_specs=[SMEM, VMEM, VMEM, VMEM, HBM],
        out_specs=[VMEM, HBM],
        out_shape=[
            pltpu.VMEM(cells.shape, jnp.bfloat16),
            jax.ShapeDtypeStruct(cells.shape, jnp.bfloat16),
        ],
        scratch_shapes=[pltpu.VMEM(cells.shape, jnp.bfloat16), DMA((CHUNKS,)), DMA((CHUNKS,))],
        cost_estimate=cost(30 * cells.size, 4 * cells.size),
        compiler_params=pltpu.CompilerParams(vmem_limit_bytes=16 << 20),
        name="transport",
    )(where, speed, signs, packet, cells)


def join_kernel(*refs):
    out_ref = refs[-1]
    for i, ref in enumerate(refs[:-1]):
        out_ref[i] = ref[0]


def join(parts):
    shape = (len(parts),) + parts[0].shape[1:]
    return pl.pallas_call(
        join_kernel,
        in_specs=[VMEM] * len(parts),
        out_specs=VMEM,
        out_shape=pltpu.VMEM(shape, parts[0].dtype),
        cost_estimate=cost(parts[0].size, 16 * parts[0].size),
        compiler_params=pltpu.CompilerParams(vmem_limit_bytes=8 << 20),
        name="join",
    )(*parts)


def collide_kernel(count, first, last, freq_ref, pair_ref, adv_ref, *refs):
    groups, refs = refs[:count], refs[count:]
    acc_ref, refs = (None, refs) if first else (refs[0], refs[1:])
    out_ref, held, in_sem = refs[:3]
    species, rows, coeffs = adv_ref.shape
    pair_count = out_ref.shape[0]
    block = rows // 2
    nt = (((1,), (1,)), ((), ()))

    def arriving(g):
        return pltpu.make_async_copy(groups[g], held.at[g], in_sem.at[g])

    def leaving(i, p):
        staged, out_sem = refs[3:]
        at = pl.ds(pl.multiple_of(i * block, block), block)
        return pltpu.make_async_copy(staged.at[p, at, :], out_ref.at[p, at, :], out_sem.at[i, p])

    def part(g, which):
        return held[g, :, which].reshape(-1, coeffs)

    for g in range(count):
        arriving(g).start()
    for t in range(count // 2):
        mine, other = 2 * t, 2 * t + 1
        arriving(mine).wait()
        arriving(other).wait()

        def step(i, carry, t=t, mine=mine, other=other):
            at = pl.ds(pl.multiple_of(i * block, block), block)
            a = adv_ref[:, at, :].reshape(species * block, coeffs)
            lefts, rights = [], []
            for g in (mine, other):
                w = jnp.concatenate([part(g, 0), part(g, 1)], axis=0)
                both = lax.dot_general(a, w, nt, preferred_element_type=jnp.float32)
                n = both.shape[1] // 2
                lefts.append(both[:, :n])
                rights.append(both[:, n:])
            left = jnp.concatenate(lefts, axis=1)
            right = jnp.concatenate(rights, axis=1)
            down = jnp.concatenate([part(mine, 2), part(other, 2)], axis=0)
            for p in range(pair_count):
                lp = jnp.where(pair_ref[0, p] == 1, left[block:], left[:block])
                rp = jnp.where(pair_ref[1, p] == 1, right[block:], right[:block])
                product = (freq_ref[p] * lp * rp).astype(jnp.bfloat16)
                term = jnp.dot(product, down, preferred_element_type=jnp.float32)
                if last:
                    refs[3][p, at, :] = (acc_ref[p, at, :] + term).astype(jnp.bfloat16)
                    leaving(i, p).start()
                    continue
                if t > 0:
                    term = out_ref[p, at, :] + term
                elif not first:
                    term = acc_ref[p, at, :] + term
                out_ref[p, at, :] = term
            return carry

        lax.fori_loop(0, 2, step, 0)
    if last:
        for i in range(2):
            for p in range(pair_count):
                leaving(i, p).wait()


def collide(adv, frequency, pairs, groups, acc, last=False):
    species, rows, coeffs = adv.shape
    pair_count = pairs.shape[1]
    ranks = sum(a.shape[0] * a.shape[2] for a in groups)
    assert not last or len(groups) == 2
    shape = (pair_count, rows, coeffs)
    operands = [frequency, pairs, adv] + groups + ([] if acc is None else [acc])
    scratch = [pltpu.VMEM((len(groups),) + groups[0].shape, jnp.bfloat16), DMA((len(groups),))]
    if last:
        scratch += [pltpu.VMEM(shape, jnp.bfloat16), DMA((2, pair_count))]
    return pl.pallas_call(
        functools.partial(collide_kernel, len(groups), acc is None, last),
        in_specs=[SMEM, SMEM, VMEM] + [ANY] * len(groups) + [VMEM] * (acc is not None),
        out_specs=HBM if last else VMEM,
        out_shape=jax.ShapeDtypeStruct(shape, jnp.bfloat16) if last else pltpu.VMEM(shape, jnp.float32),
        scratch_shapes=scratch,
        input_output_aliases={} if acc is None or last else {len(operands) - 1: 0},
        cost_estimate=cost(
            2 * ranks * coeffs * rows * (2 * species + pair_count),
            2 * (adv.size + 3 * ranks * coeffs),
        ),
        compiler_params=pltpu.CompilerParams(vmem_limit_bytes=30 << 20),
        name="collide",
    )(*operands)


def phase(mine):
    return [mine, send(mine, UP1), send(mine, DOWN1), send(mine, FAR1)]


def swap(array):
    return send(array, PARTNER)


def after(array, *others):
    return lax.optimization_barrier((array,) + others)[0]


def local(distribution, face_signs, stream_speed, factors, pair_list, frequency):
    species, lines, cells, coeffs = distribution.shape
    here = lax.axis_index("space").astype(jnp.int32)[None]
    mine = factors[None]
    signs, pairs = face_signs.T, pair_list.T

    parts_o = phase(mine)
    cross = send(mine, CROSS)
    packet = packet_of(distribution, signs, here)
    got = send(packet, SIDE)
    parts_o[0] = after(mine, packet)
    group_o = join(parts_o)
    up_o, down_o, swap_o = send(group_o, UP2), send(group_o, DOWN2), swap(group_o)

    parts_c = phase(after(cross, group_o))
    adv_near, advanced = transport(distribution, got, signs, stream_speed[None], here)
    parts_c[0] = after(parts_c[0], adv_near)
    group_c = join(parts_c)
    up_c, down_c, swap_c = send(group_c, UP2), send(group_c, DOWN2), swap(group_c)

    adv = adv_near.reshape(species, lines * cells, coeffs)
    step = functools.partial(collide, adv, frequency, pairs)

    acc = step([after(group_o, group_c), swap_o], None)
    far_o = send(after(up_o, acc), UP2)
    acc = step([up_o, swap(up_o), down_o, swap(down_o), group_c, swap_c], acc)
    far_c = send(after(down_c, acc), DOWN2)
    acc = step([far_o, swap(far_o)], acc)
    acc = step([down_c, swap(down_c)], acc)
    acc = step([up_c, swap(up_c)], acc)
    out = step([far_c, swap(far_c)], acc, last=True)
    collision = out.reshape(pair_list.shape[0], lines, cells, coeffs)
    return (advanced, collision)


def solution(mesh):
    return jax.shard_map(
        local,
        mesh=mesh,
        in_specs=(
            P(None, "blk", "space", None),
            P("blk", "space"),
            P(),
            P(None, "blk", None),
            P(),
            P(),
        ),
        out_specs=(P(None, "blk", "space", None), P(None, "blk", "space", None)),
        check_vma=False,
    )
```

```python
import functools
import jax
import jax.numpy as jnp
from jax import lax
from jax.experimental import pallas as pl
from jax.experimental.pallas import tpu as pltpu
from jax.sharding import PartitionSpec as P

courant = 0.3
AXES = ("blk", "space")
SIZES = (4, 4, 4, 2)


def flat_index(z, y, x, core):
    return (((z * 2 + y // 2) * 4 + x) * 2 + core) * 2 + y % 2


def pairs_of(move):
    pairs = []
    for z in range(4):
        for y in range(4):
            for x in range(4):
                for core in range(2):
                    target = [v % n for v, n in zip(move(z, y, x, core), SIZES)]
                    pairs.append((flat_index(z, y, x, core), flat_index(*target)))
    return pairs


def along(step, first):
    return pairs_of(
        lambda z, y, x, core: (z, y, x + step, core)
        if (core == 0) == first
        else (z + step, y, x, core)
    )


PARTNER = pairs_of(lambda z, y, x, core: (z, y, x, 1 - core))
CROSS = pairs_of(lambda z, y, x, core: (z, 3 - y, x, core))
SIDE = pairs_of(lambda z, y, x, core: (z, y ^ 1, x, core))
UP1, DOWN1, FAR1 = along(1, True), along(-1, True), along(2, True)
UP2, DOWN2 = along(1, False), along(-1, False)


SMEM = pl.BlockSpec(memory_space=pltpu.SMEM)
HBM = pl.BlockSpec(memory_space=pltpu.HBM)
VMEM = pl.BlockSpec(memory_space=pltpu.VMEM)
DMA = pltpu.SemaphoreType.DMA


def cost(flops, moved):
    return pl.CostEstimate(flops=flops, bytes_accessed=moved, transcendentals=0)


def stay(array):
    return pltpu.with_memory_space_constraint(array, pltpu.HBM)


def packet_kernel(where_ref, signs_hbm, cells_ref, out_ref, rows, signs_ref, sem, sign_sem):
    first_part = where_ref[0] == 0
    species, lines, cells, coeffs = cells_ref.shape
    start = pl.multiple_of(jnp.where(first_part, cells - 8, 0), 8)
    copy = pltpu.make_async_copy(cells_ref.at[:, :, pl.ds(start, 8), :], rows, sem)
    copy.start()
    sign_copy = pltpu.make_async_copy(signs_hbm, signs_ref, sign_sem)
    sign_copy.start()
    out_ref[species * lines] = jnp.zeros((2, coeffs), jnp.bfloat16)
    sign_copy.wait()
    last = signs_ref[cells - 1 : cells, :].astype(jnp.float32)
    last = jnp.concatenate([last, last], axis=0).astype(jnp.bfloat16)
    out_ref[species * lines, :, 0:lines] = last
    copy.wait()

    def one(l, carry):
        for s in range(species):
            eight = rows[s, l].astype(jnp.float32)
            edge = jnp.where(first_part, eight[6:8], eight[0:2])
            out_ref[s * lines + l] = edge.astype(jnp.bfloat16)
        return carry

    lax.fori_loop(0, lines, one, 0)


def packet_of(cells, signs, where):
    species, lines, _, coeffs = cells.shape
    return pl.pallas_call(
        packet_kernel,
        in_specs=[SMEM, HBM, HBM],
        out_specs=VMEM,
        out_shape=jax.ShapeDtypeStruct((species * lines + 1, 2, coeffs), jnp.bfloat16),
        scratch_shapes=[
            pltpu.VMEM((species, lines, 8, coeffs), jnp.bfloat16),
            pltpu.VMEM(signs.shape, jnp.int32),
            DMA,
            DMA,
        ],
        cost_estimate=cost(cells.size, cells.size),
        compiler_params=pltpu.CompilerParams(vmem_limit_bytes=8 << 20),
        name="packet",
    )(where, stay(signs), stay(cells))


CHUNKS = 4


def transport_kernel(where_ref, speed_ref, signs_ref, packet_ref, cells_hbm, out_ref, out_hbm, cells_ref, in_sem, out_sem):
    first_part = where_ref[0] == 0
    species, lines, cells, coeffs = cells_ref.shape
    chunk = lines // CHUNKS

    def arriving(c):
        at = pl.ds(c * chunk, chunk)
        return pltpu.make_async_copy(cells_hbm.at[:, at], cells_ref.at[:, at], in_sem.at[c])

    def leaving(c):
        at = pl.ds(c * chunk, chunk)
        return pltpu.make_async_copy(out_ref.at[:, at], out_hbm.at[:, at], out_sem.at[c])

    for c in range(CHUNKS):
        arriving(c).start()
    width = 512
    row = lax.broadcasted_iota(jnp.int32, (cells, width), 0)
    row1 = lax.broadcasted_iota(jnp.int32, (cells, lines), 0)
    lane = lax.broadcasted_iota(jnp.int32, (cells, lines), 1)
    signs = (2 * signs_ref[...] - 1).astype(jnp.float32)
    signs = jnp.where(jnp.logical_and(row1 == cells - 1, jnp.logical_not(first_part)), 0.0, signs)
    got = 2.0 * packet_ref[species * lines, 0:1, 0:lines].astype(jnp.float32) - 1.0
    got = jnp.where(first_part, 0.0, got)

    def one(l, carry):
        d_right = jnp.sum(jnp.where(lane == l, signs, 0.0), axis=1, keepdims=True)
        d_first = jnp.sum(jnp.where(lane[0:1] == l, got, 0.0), axis=1, keepdims=True)
        d_right = jnp.broadcast_to(d_right, (cells, width))
        d_first = jnp.broadcast_to(d_first, (1, width))
        for c in range(coeffs // width):
            at = slice(c * width, (c + 1) * width)
            speed = speed_ref[:, at]
            for s in range(species):
                f = cells_ref[s, l, :, at].astype(jnp.float32)
                halo = packet_ref[s * lines + l, :, at].astype(jnp.float32)
                h0, h1 = halo[0:1], halo[1:2]
                zero = jnp.zeros_like(h0)
                left2, left1 = jnp.where(first_part, zero, h0), jnp.where(first_part, zero, h1)
                right1, right2 = jnp.where(first_part, h0, zero), jnp.where(first_part, h1, zero)
                before = jnp.where(row == 0, left1, pltpu.roll(f, 1, 0))
                after = jnp.where(row == cells - 1, right1, pltpu.roll(f, cells - 1, 0))
                upper = f + 0.5 * (f - before)
                lower = f - 0.5 * (after - f)
                lower_last = right1 - 0.5 * (right2 - right1)
                lower_next = jnp.where(row == cells - 1, lower_last, pltpu.roll(lower, cells - 1, 0))
                flux = d_right * speed * jnp.where(d_right > 0, upper, lower_next)
                upper_first = left1 + 0.5 * (left1 - left2)
                flux_first = d_first * speed * jnp.where(d_first > 0, upper_first, lower[0:1])
                flux_before = jnp.where(row == 0, flux_first, pltpu.roll(flux, 1, 0))
                out_ref[s, l, :, at] = (f - courant * (flux - flux_before)).astype(jnp.bfloat16)
        return carry

    for c in range(CHUNKS):
        arriving(c).wait()
        lax.fori_loop(c * chunk, (c + 1) * chunk, one, 0)
        leaving(c).start()
    for c in range(CHUNKS):
        leaving(c).wait()


def transport(cells, packet, signs, speed, where):
    return pl.pallas_call(
        transport_kernel,
        in_specs=[SMEM, VMEM, VMEM, VMEM, HBM],
        out_specs=[VMEM, HBM],
        out_shape=[
            pltpu.VMEM(cells.shape, jnp.bfloat16),
            jax.ShapeDtypeStruct(cells.shape, jnp.bfloat16),
        ],
        scratch_shapes=[pltpu.VMEM(cells.shape, jnp.bfloat16), DMA((CHUNKS,)), DMA((CHUNKS,))],
        cost_estimate=cost(30 * cells.size, 4 * cells.size),
        compiler_params=pltpu.CompilerParams(vmem_limit_bytes=16 << 20),
        name="transport",
    )(where, speed, signs, packet, stay(cells))


def join_kernel(*refs):
    out_ref = refs[-1]
    for i, ref in enumerate(refs[:-1]):
        out_ref[i] = ref[0]


def join(parts):
    shape = (len(parts),) + parts[0].shape[1:]
    return pl.pallas_call(
        join_kernel,
        in_specs=[VMEM] * len(parts),
        out_specs=VMEM,
        out_shape=pltpu.VMEM(shape, parts[0].dtype),
        cost_estimate=cost(parts[0].size, 16 * parts[0].size),
        compiler_params=pltpu.CompilerParams(vmem_limit_bytes=8 << 20),
        name="join",
    )(*parts)


def collide_kernel(count, first, last, freq_ref, pair_ref, adv_ref, *refs):
    groups, refs = refs[:count], refs[count:]
    acc_ref, refs = (None, refs) if first else (refs[0], refs[1:])
    out_ref = refs[0]
    species, rows, coeffs = adv_ref.shape
    pair_count = out_ref.shape[0]
    block = rows // 2
    nt = (((1,), (1,)), ((), ()))

    def leaving(i, p):
        staged, out_sem = refs[1:]
        at = pl.ds(pl.multiple_of(i * block, block), block)
        return pltpu.make_async_copy(staged.at[p, at, :], out_ref.at[p, at, :], out_sem.at[i, p])

    def part(g, which):
        return groups[g][:, which].reshape(-1, coeffs)

    for t in range(count // 2):
        mine, other = 2 * t, 2 * t + 1

        def step(i, carry, t=t, mine=mine, other=other):
            at = pl.ds(pl.multiple_of(i * block, block), block)
            a = adv_ref[:, at, :].reshape(species * block, coeffs)
            lefts, rights = [], []
            for g in (mine, other):
                w = jnp.concatenate([part(g, 0), part(g, 1)], axis=0)
                both = lax.dot_general(a, w, nt, preferred_element_type=jnp.float32)
                n = both.shape[1] // 2
                lefts.append(both[:, :n])
                rights.append(both[:, n:])
            left = jnp.concatenate(lefts, axis=1)
            right = jnp.concatenate(rights, axis=1)
            down = jnp.concatenate([part(mine, 2), part(other, 2)], axis=0)
            for p in range(pair_count):
                lp = jnp.where(pair_ref[0, p] == 1, left[block:], left[:block])
                rp = jnp.where(pair_ref[1, p] == 1, right[block:], right[:block])
                product = (freq_ref[p] * lp * rp).astype(jnp.bfloat16)
                term = jnp.dot(product, down, preferred_element_type=jnp.float32)
                if last:
                    refs[1][p, at, :] = (acc_ref[p, at, :] + term).astype(jnp.bfloat16)
                    leaving(i, p).start()
                    continue
                if t > 0:
                    term = out_ref[p, at, :] + term
                elif not first:
                    term = acc_ref[p, at, :] + term
                out_ref[p, at, :] = term
            return carry

        lax.fori_loop(0, 2, step, 0)
    if last:
        for i in range(2):
            for p in range(pair_count):
                leaving(i, p).wait()


def collide(adv, frequency, pairs, groups, acc, last=False):
    species, rows, coeffs = adv.shape
    pair_count = pairs.shape[1]
    ranks = sum(a.shape[0] * a.shape[2] for a in groups)
    assert not last or len(groups) == 2
    shape = (pair_count, rows, coeffs)
    operands = [frequency, pairs, adv] + groups + ([] if acc is None else [acc])
    scratch = []
    if last:
        scratch = [pltpu.VMEM(shape, jnp.bfloat16), DMA((2, pair_count))]
    return pl.pallas_call(
        functools.partial(collide_kernel, len(groups), acc is None, last),
        in_specs=[SMEM, SMEM] + [VMEM] * (len(operands) - 2),
        out_specs=HBM if last else VMEM,
        out_shape=jax.ShapeDtypeStruct(shape, jnp.bfloat16) if last else pltpu.VMEM(shape, jnp.float32),
        scratch_shapes=scratch,
        input_output_aliases={} if acc is None or last else {len(operands) - 1: 0},
        cost_estimate=cost(
            2 * ranks * coeffs * rows * (2 * species + pair_count),
            2 * (adv.size + 3 * ranks * coeffs),
        ),
        compiler_params=pltpu.CompilerParams(vmem_limit_bytes=20 << 20),
        name="collide",
    )(*operands)


def send(array, pairs):
    return lax.ppermute(array, AXES, pairs)


def phase(mine):
    return [mine, send(mine, UP1), send(mine, DOWN1), send(mine, FAR1)]


def after(array, *others):
    return lax.optimization_barrier((array,) + others)[0]


def local(distribution, face_signs, stream_speed, factors, pair_list, frequency):
    species, lines, cells, coeffs = distribution.shape
    here = lax.axis_index("space").astype(jnp.int32)[None]
    mine = factors[None]
    signs, pairs = face_signs.T, pair_list.T

    cross = send(mine, CROSS)
    parts_o = phase(mine)
    packet = packet_of(distribution, signs, here)
    got = send(packet, SIDE)
    parts_o[0] = after(mine, packet)
    group_o = join(parts_o)
    up_o, down_o = send(group_o, UP2), send(group_o, DOWN2)
    swap_o = send(group_o, PARTNER)

    parts_c = phase(after(cross, group_o))
    adv_near, advanced = transport(distribution, got, signs, stream_speed[None], here)
    parts_c[0] = after(parts_c[0], adv_near)
    group_c = join(parts_c)
    up_c, down_c = send(group_c, UP2), send(group_c, DOWN2)
    swap_c = send(group_c, PARTNER)

    adv = adv_near.reshape(species, lines * cells, coeffs)

    def step(groups, acc, last=False):
        return collide(adv, frequency, pairs, groups, acc, last)

    acc = step([after(group_o, group_c), swap_o], None)
    acc = step([group_c, swap_c], acc)
    up_o, down_o, _ = lax.optimization_barrier((up_o, down_o, acc))
    far_o = send(up_o, UP2)
    acc = step([up_o, send(up_o, PARTNER), down_o, send(down_o, PARTNER)], acc)
    down_c = after(down_c, acc)
    far_c = send(down_c, DOWN2)
    acc = step([down_c, send(down_c, PARTNER)], acc)
    far_o = after(far_o, acc)
    acc = step([far_o, send(far_o, PARTNER)], acc)
    up_c = after(up_c, acc)
    acc = step([up_c, send(up_c, PARTNER)], acc)
    out = step([far_c, send(far_c, PARTNER)], acc, last=True)
    collision = out.reshape(pair_list.shape[0], lines, cells, coeffs)
    return (advanced, collision)


def solution(mesh):
    return jax.shard_map(
        local,
        mesh=mesh,
        in_specs=(
            P(None, "blk", "space", None),
            P("blk", "space"),
            P(),
            P(None, "blk", None),
            P(),
            P(),
        ),
        out_specs=(P(None, "blk", "space", None), P(None, "blk", "space", None)),
        check_vma=False,
    )
```

```python
import functools
import jax
import jax.numpy as jnp
from jax import lax
from jax.experimental import pallas as pl
from jax.experimental.pallas import tpu as pltpu
from jax.sharding import PartitionSpec as P

courant = 0.3
AXES = ("blk", "space")
SIZES = (4, 4, 4, 2)


def flat_index(z, y, x, core):
    return (((z * 2 + y // 2) * 4 + x) * 2 + core) * 2 + y % 2


def pairs_of(move):
    pairs = []
    for z in range(4):
        for y in range(4):
            for x in range(4):
                for core in range(2):
                    target = [v % n for v, n in zip(move(z, y, x, core), SIZES)]
                    pairs.append((flat_index(z, y, x, core), flat_index(*target)))
    return pairs


def along(step, first):
    return pairs_of(
        lambda z, y, x, core: (z, y, x + step, core)
        if (core == 0) == first
        else (z + step, y, x, core)
    )


PARTNER = pairs_of(lambda z, y, x, core: (z, y, x, 1 - core))
CROSS = pairs_of(lambda z, y, x, core: (z, 3 - y, x, core))
SIDE = pairs_of(lambda z, y, x, core: (z, y ^ 1, x, core))
UP1, DOWN1, FAR1 = along(1, True), along(-1, True), along(2, True)
UP2, DOWN2 = along(1, False), along(-1, False)


SMEM = pl.BlockSpec(memory_space=pltpu.SMEM)
HBM = pl.BlockSpec(memory_space=pltpu.HBM)
VMEM = pl.BlockSpec(memory_space=pltpu.VMEM)
DMA = pltpu.SemaphoreType.DMA


def cost(flops, moved):
    return pl.CostEstimate(flops=flops, bytes_accessed=moved, transcendentals=0)


def stay(array):
    return pltpu.with_memory_space_constraint(array, pltpu.HBM)


def packet_kernel(where_ref, signs_hbm, cells_ref, out_ref, rows, edges, signs_ref, sem, sign_sem):
    first_part = where_ref[0] == 0
    species, lines, cells, coeffs = cells_ref.shape
    start = pl.multiple_of(jnp.where(first_part, cells - 8, 0), 8)
    copy = pltpu.make_async_copy(cells_ref.at[:, :, pl.ds(start, 8), :], rows, sem)
    copy.start()
    sign_copy = pltpu.make_async_copy(signs_hbm, signs_ref, sign_sem)
    sign_copy.start()
    total = species * lines
    edges[:, total:, :] = jnp.zeros((2, 8, coeffs), jnp.float32)
    sign_copy.wait()
    edges[0, total : total + 1, 0:lines] = signs_ref[cells - 1 : cells, :].astype(jnp.float32)
    copy.wait()

    def one(l, carry):
        for s in range(species):
            eight = rows[s, l].astype(jnp.float32)
            at = pl.ds(s * lines + l, 1)
            edges[0, at, :] = jnp.where(first_part, eight[6:7], eight[0:1])
            edges[1, at, :] = jnp.where(first_part, eight[7:8], eight[1:2])
        return carry

    lax.fori_loop(0, lines, one, 0)
    out_ref[...] = edges[...].astype(jnp.bfloat16)


def packet_of(cells, signs, where):
    species, lines, _, coeffs = cells.shape
    shape = (2, species * lines + 8, coeffs)
    return pl.pallas_call(
        packet_kernel,
        in_specs=[SMEM, HBM, HBM],
        out_specs=VMEM,
        out_shape=jax.ShapeDtypeStruct(shape, jnp.bfloat16),
        scratch_shapes=[
            pltpu.VMEM((species, lines, 8, coeffs), jnp.bfloat16),
            pltpu.VMEM(shape, jnp.float32),
            pltpu.VMEM(signs.shape, jnp.int32),
            DMA,
            DMA,
        ],
        cost_estimate=cost(cells.size, cells.size),
        compiler_params=pltpu.CompilerParams(vmem_limit_bytes=10 << 20),
        name="packet",
    )(where, stay(signs), stay(cells))


CHUNKS = 4


def transport_kernel(
    where_ref, speed_ref, signs_ref, packet_ref, cells_hbm, out_ref, out_hbm, cells_ref, sides, dirs, in_sem, out_sem
):
    first_part = where_ref[0] == 0
    species, lines, cells, coeffs = cells_ref.shape
    chunk = lines // CHUNKS
    total = species * lines

    def arriving(c):
        at = pl.ds(c * chunk, chunk)
        return pltpu.make_async_copy(cells_hbm.at[:, at], cells_ref.at[:, at], in_sem.at[c])

    def leaving(c):
        at = pl.ds(c * chunk, chunk)
        return pltpu.make_async_copy(out_ref.at[:, at], out_hbm.at[:, at], out_sem.at[c])

    for c in range(CHUNKS):
        arriving(c).start()

    column = lax.broadcasted_iota(jnp.int32, (cells, lines), 0)
    signs = (2 * signs_ref[...] - 1).astype(jnp.float32)
    signs = jnp.where(jnp.logical_and(column == cells - 1, jnp.logical_not(first_part)), 0.0, signs)
    got = 2.0 * packet_ref[0, total : total + 8, 0:lines].astype(jnp.float32) - 1.0
    got = jnp.where(first_part, 0.0, got)
    for l in range(lines):
        dirs[l, 0] = jnp.broadcast_to(signs[0:8, l : l + 1], (8, 128))
        dirs[l, 1] = jnp.broadcast_to(signs[8:16, l : l + 1], (8, 128))
        dirs[l, 2] = jnp.broadcast_to(got[0:1, l : l + 1], (8, 128))

    def side(t, carry):
        at = pl.ds(pl.multiple_of(t * 128, 128), 128)
        h0 = packet_ref[0, :, at].astype(jnp.float32)[0:total]
        h1 = packet_ref[1, :, at].astype(jnp.float32)[0:total]
        zero = jnp.zeros_like(h0)
        sides[0, t, 0:total] = jnp.where(first_part, zero, h1)
        sides[1, t, 0:total] = jnp.where(first_part, h0, zero)
        sides[2, t, 0:total] = jnp.where(first_part, h0 - 0.5 * (h1 - h0), h1 + 0.5 * (h1 - h0))
        sides[3, t, 0:total] = jnp.where(first_part, h1 - h0, zero)
        return carry

    lax.fori_loop(0, coeffs // 128, side, 0)
    row = lax.broadcasted_iota(jnp.int32, (8, 128), 0)
    top, bottom = row == 0, row == 7

    def down(low, high, edge):
        low_r, high_r = pltpu.roll(low, 1, 0), pltpu.roll(high, 1, 0)
        return jnp.where(top, edge, low_r), jnp.where(top, low_r, high_r)

    def up(low, high, edge):
        low_r, high_r = pltpu.roll(low, 7, 0), pltpu.roll(high, 7, 0)
        return jnp.where(bottom, high_r, low_r), jnp.where(bottom, edge, high_r)

    def one(l, carry):
        d0, d1, df = dirs[l, 0], dirs[l, 1], dirs[l, 2]
        p0, p1, pf = d0 > 0, d1 > 0, df > 0
        for c in range(coeffs // 128):
            at = slice(c * 128, (c + 1) * 128)
            speed = jnp.broadcast_to(speed_ref[:, at], (8, 128))
            v0, v1, vf = d0 * speed, d1 * speed, df * speed
            for s in range(species):
                f = cells_ref[s, l, :, at].astype(jnp.float32)
                f0, f1 = f[0:8], f[8:16]
                left, right, ext, diff = (
                    sides[k, c, pl.ds(s * lines + l, 8, stride=0), :] for k in range(4)
                )
                a0, a1 = up(f0, f1, right)
                b0, b1 = down(f0, f1, left)
                n0, n1 = a0 - f0, a1 - f1
                m0, m1 = up(n0, n1, diff)
                upper0, upper1 = f0 + 0.5 * (f0 - b0), f1 + 0.5 * (f1 - b1)
                lower0, lower1 = a0 - 0.5 * m0, a1 - 0.5 * m1
                flux0 = v0 * jnp.where(p0, upper0, lower0)
                flux1 = v1 * jnp.where(p1, upper1, lower1)
                first = vf * jnp.where(pf, ext, f0 - 0.5 * n0)
                g0, g1 = down(flux0, flux1, first)
                new = jnp.concatenate([f0 - courant * (flux0 - g0), f1 - courant * (flux1 - g1)], axis=0)
                out_ref[s, l, :, at] = new.astype(jnp.bfloat16)
        return carry

    for c in range(CHUNKS):
        arriving(c).wait()
        lax.fori_loop(c * chunk, (c + 1) * chunk, one, 0)
        leaving(c).start()
    for c in range(CHUNKS):
        leaving(c).wait()


def transport(cells, packet, signs, speed, where):
    species, lines, _, coeffs = cells.shape
    return pl.pallas_call(
        transport_kernel,
        in_specs=[SMEM, VMEM, VMEM, VMEM, HBM],
        out_specs=[VMEM, HBM],
        out_shape=[
            pltpu.VMEM(cells.shape, jnp.bfloat16),
            jax.ShapeDtypeStruct(cells.shape, jnp.bfloat16),
        ],
        scratch_shapes=[
            pltpu.VMEM(cells.shape, jnp.bfloat16),
            pltpu.VMEM((4, coeffs // 128, species * lines + 8, 128), jnp.float32),
            pltpu.VMEM((cells.shape[1], 3, 8, 128), jnp.float32),
            DMA((CHUNKS,)),
            DMA((CHUNKS,)),
        ],
        cost_estimate=cost(30 * cells.size, 4 * cells.size),
        compiler_params=pltpu.CompilerParams(vmem_limit_bytes=16 << 20),
        name="transport",
    )(where, speed, signs, packet, stay(cells))


def join_kernel(*refs):
    out_ref = refs[-1]
    for i, ref in enumerate(refs[:-1]):
        out_ref[i] = ref[0]


def join(parts):
    shape = (len(parts),) + parts[0].shape[1:]
    return pl.pallas_call(
        join_kernel,
        in_specs=[VMEM] * len(parts),
        out_specs=VMEM,
        out_shape=pltpu.VMEM(shape, parts[0].dtype),
        cost_estimate=cost(parts[0].size, 16 * parts[0].size),
        compiler_params=pltpu.CompilerParams(vmem_limit_bytes=8 << 20),
        name="join",
    )(*parts)


def collide_kernel(count, first, last, freq_ref, pair_ref, adv_ref, *refs):
    groups, refs = refs[:count], refs[count:]
    acc_ref, refs = (None, refs) if first else (refs[0], refs[1:])
    out_ref = refs[0]
    species, rows, coeffs = adv_ref.shape
    pair_count = out_ref.shape[0]
    blocks = 2 if last else 1
    block = rows // blocks
    nt = (((1,), (1,)), ((), ()))

    def leaving(i, p):
        staged, out_sem = refs[1:]
        at = pl.ds(pl.multiple_of(i * block, block), block)
        return pltpu.make_async_copy(staged.at[p, at, :], out_ref.at[p, at, :], out_sem.at[i, p])

    def part(g, which):
        return groups[g][:, which].reshape(-1, coeffs)

    for t in range(count // 2):
        mine, other = 2 * t, 2 * t + 1

        def step(i, carry, t=t, mine=mine, other=other):
            at = pl.ds(pl.multiple_of(i * block, block), block)
            a = adv_ref[:, at, :].reshape(species * block, coeffs)
            lefts, rights = [], []
            for g in (mine, other):
                w = jnp.concatenate([part(g, 0), part(g, 1)], axis=0)
                both = lax.dot_general(a, w, nt, preferred_element_type=jnp.float32)
                n = both.shape[1] // 2
                lefts.append(both[:, :n])
                rights.append(both[:, n:])
            left = jnp.concatenate(lefts, axis=1)
            right = jnp.concatenate(rights, axis=1)
            down = jnp.concatenate([part(mine, 2), part(other, 2)], axis=0)
            for p in range(pair_count):
                lp = jnp.where(pair_ref[0, p] == 1, left[block:], left[:block])
                rp = jnp.where(pair_ref[1, p] == 1, right[block:], right[:block])
                product = (freq_ref[p] * lp * rp).astype(jnp.bfloat16)
                term = jnp.dot(product, down, preferred_element_type=jnp.float32)
                if last:
                    refs[1][p, at, :] = (acc_ref[p, at, :] + term).astype(jnp.bfloat16)
                    leaving(i, p).start()
                    continue
                if t > 0:
                    term = out_ref[p, at, :] + term
                elif not first:
                    term = acc_ref[p, at, :] + term
                out_ref[p, at, :] = term
            return carry

        lax.fori_loop(0, blocks, step, 0)
    if last:
        for i in range(blocks):
            for p in range(pair_count):
                leaving(i, p).wait()


def collide(adv, frequency, pairs, groups, acc, last=False):
    species, rows, coeffs = adv.shape
    pair_count = pairs.shape[1]
    ranks = sum(a.shape[0] * a.shape[2] for a in groups)
    assert not last or len(groups) == 2
    shape = (pair_count, rows, coeffs)
    operands = [frequency, pairs, adv] + groups + ([] if acc is None else [acc])
    scratch = []
    if last:
        scratch = [pltpu.VMEM(shape, jnp.bfloat16), DMA((2, pair_count))]
    return pl.pallas_call(
        functools.partial(collide_kernel, len(groups), acc is None, last),
        in_specs=[SMEM, SMEM] + [VMEM] * (len(operands) - 2),
        out_specs=HBM if last else VMEM,
        out_shape=jax.ShapeDtypeStruct(shape, jnp.bfloat16) if last else pltpu.VMEM(shape, jnp.float32),
        scratch_shapes=scratch,
        input_output_aliases={} if acc is None or last else {len(operands) - 1: 0},
        cost_estimate=cost(
            2 * ranks * coeffs * rows * (2 * species + pair_count),
            2 * (adv.size + 3 * ranks * coeffs),
        ),
        compiler_params=pltpu.CompilerParams(vmem_limit_bytes=20 << 20),
        name="collide",
    )(*operands)


def send(array, pairs):
    return lax.ppermute(array, AXES, pairs)


def phase(mine):
    return [mine, send(mine, UP1), send(mine, DOWN1), send(mine, FAR1)]


def after(array, *others):
    return lax.optimization_barrier((array,) + others)[0]


def local(distribution, face_signs, stream_speed, factors, pair_list, frequency):
    species, lines, cells, coeffs = distribution.shape
    here = lax.axis_index("space").astype(jnp.int32)[None]
    mine = factors[None]
    signs, pairs = face_signs.T, pair_list.T

    cross = send(mine, CROSS)
    parts_o = phase(mine)
    parts_c = phase(cross)
    packet = packet_of(distribution, signs, here)
    got = send(packet, SIDE)
    parts_o[0] = after(mine, packet)
    group_o = join(parts_o)
    up_o, down_o = send(group_o, UP2), send(group_o, DOWN2)
    swap_o = send(group_o, PARTNER)
    adv_near, advanced = transport(distribution, got, signs, stream_speed[None], here)
    parts_c[0] = after(parts_c[0], adv_near)
    group_c = join(parts_c)
    up_c, down_c = send(group_c, UP2), send(group_c, DOWN2)
    swap_c = send(group_c, PARTNER)

    adv = adv_near.reshape(species, lines * cells, coeffs)

    def step(groups, acc, last=False):
        return collide(adv, frequency, pairs, groups, acc, last)

    acc = step([after(group_o, group_c), swap_o], None)
    acc = step([group_c, swap_c], acc)
    up_o, down_o, _ = lax.optimization_barrier((up_o, down_o, acc))
    far_o = send(up_o, UP2)
    swap_uo, swap_do = send(up_o, PARTNER), send(down_o, PARTNER)
    acc = step([up_o, swap_uo, down_o, swap_do], acc)
    down_c, up_c, _ = lax.optimization_barrier((down_c, up_c, acc))
    far_c = send(down_c, DOWN2)
    swap_dc, swap_uc = send(down_c, PARTNER), send(up_c, PARTNER)
    acc = step([down_c, up_c], acc)
    acc = step([swap_dc, swap_uc], acc)
    far_o, far_c, _ = lax.optimization_barrier((far_o, far_c, acc))
    swap_fo, swap_fc = send(far_o, PARTNER), send(far_c, PARTNER)
    acc = step([far_o, far_c], acc)
    out = step([swap_fo, swap_fc], acc, last=True)
    collision = out.reshape(pair_list.shape[0], lines, cells, coeffs)
    return (advanced, collision)


def solution(mesh):
    return jax.shard_map(
        local,
        mesh=mesh,
        in_specs=(
            P(None, "blk", "space", None),
            P("blk", "space"),
            P(),
            P(None, "blk", None),
            P(),
            P(),
        ),
        out_specs=(P(None, "blk", "space", None), P(None, "blk", "space", None)),
        check_vma=False,
    )
```

```python
import functools
import jax
import jax.numpy as jnp
from jax import lax
from jax.experimental import pallas as pl
from jax.experimental.pallas import tpu as pltpu
from jax.sharding import PartitionSpec as P

courant = 0.3
AXES = ("blk", "space")
SIZES = (4, 4, 4, 2)


def flat_index(z, y, x, core):
    return (((z * 2 + y // 2) * 4 + x) * 2 + core) * 2 + y % 2


def pairs_of(move):
    pairs = []
    for z in range(4):
        for y in range(4):
            for x in range(4):
                for core in range(2):
                    target = [v % n for v, n in zip(move(z, y, x, core), SIZES)]
                    pairs.append((flat_index(z, y, x, core), flat_index(*target)))
    return pairs


def along(step, first):
    return pairs_of(
        lambda z, y, x, core: (z, y, x + step, core)
        if (core == 0) == first
        else (z + step, y, x, core)
    )


PARTNER = pairs_of(lambda z, y, x, core: (z, y, x, 1 - core))
CROSS = pairs_of(lambda z, y, x, core: (z, 3 - y, x, core))
SIDE = pairs_of(lambda z, y, x, core: (z, y ^ 1, x, core))
UP1, DOWN1, FAR1 = along(1, True), along(-1, True), along(2, True)
UP2, DOWN2 = along(1, False), along(-1, False)


SMEM = pl.BlockSpec(memory_space=pltpu.SMEM)
HBM = pl.BlockSpec(memory_space=pltpu.HBM)
VMEM = pl.BlockSpec(memory_space=pltpu.VMEM)
DMA = pltpu.SemaphoreType.DMA


def cost(flops, moved):
    return pl.CostEstimate(flops=flops, bytes_accessed=moved, transcendentals=0)


def stay(array):
    return pltpu.with_memory_space_constraint(array, pltpu.HBM)


def packet_kernel(where_ref, signs_hbm, cells_ref, out_ref, rows, edges, signs_ref, sem, sign_sem):
    first_part = where_ref[0] == 0
    species, lines, cells, coeffs = cells_ref.shape
    start = pl.multiple_of(jnp.where(first_part, cells - 8, 0), 8)
    copy = pltpu.make_async_copy(cells_ref.at[:, :, pl.ds(start, 8), :], rows, sem)
    copy.start()
    sign_copy = pltpu.make_async_copy(signs_hbm, signs_ref, sign_sem)
    sign_copy.start()
    total = species * lines
    edges[:, total:, :] = jnp.zeros((2, 8, coeffs), jnp.float32)
    sign_copy.wait()
    edges[0, total : total + 1, 0:lines] = signs_ref[cells - 1 : cells, :].astype(jnp.float32)
    copy.wait()

    def one(l, carry):
        for s in range(species):
            eight = rows[s, l].astype(jnp.float32)
            at = pl.ds(s * lines + l, 1)
            edges[0, at, :] = jnp.where(first_part, eight[6:7], eight[0:1])
            edges[1, at, :] = jnp.where(first_part, eight[7:8], eight[1:2])
        return carry

    lax.fori_loop(0, lines, one, 0)
    out_ref[...] = edges[...].astype(jnp.bfloat16)


def packet_of(cells, signs, where):
    species, lines, _, coeffs = cells.shape
    shape = (2, species * lines + 8, coeffs)
    return pl.pallas_call(
        packet_kernel,
        in_specs=[SMEM, HBM, HBM],
        out_specs=VMEM,
        out_shape=jax.ShapeDtypeStruct(shape, jnp.bfloat16),
        scratch_shapes=[
            pltpu.VMEM((species, lines, 8, coeffs), jnp.bfloat16),
            pltpu.VMEM(shape, jnp.float32),
            pltpu.VMEM(signs.shape, jnp.int32),
            DMA,
            DMA,
        ],
        cost_estimate=cost(cells.size, cells.size),
        compiler_params=pltpu.CompilerParams(vmem_limit_bytes=10 << 20),
        name="packet",
    )(where, stay(signs), stay(cells))


CHUNKS = 7


def transport_kernel(
    where_ref, speed_ref, signs_ref, packet_ref, cells_hbm, out_ref, out_hbm, cells_ref, sides, dirs, in_sem, out_sem
):
    first_part = where_ref[0] == 0
    species, lines, cells, coeffs = cells_ref.shape
    chunk = lines // CHUNKS
    total = species * lines

    def arriving(c):
        at = pl.ds(c * chunk, chunk)
        return pltpu.make_async_copy(cells_hbm.at[:, at], cells_ref.at[:, at], in_sem.at[c])

    def leaving(c):
        at = pl.ds(c * chunk, chunk)
        return pltpu.make_async_copy(out_ref.at[:, at], out_hbm.at[:, at], out_sem.at[c])

    for c in range(CHUNKS):
        arriving(c).start()

    column = lax.broadcasted_iota(jnp.int32, (cells, lines), 0)
    signs = (2 * signs_ref[...] - 1).astype(jnp.float32)
    signs = jnp.where(jnp.logical_and(column == cells - 1, jnp.logical_not(first_part)), 0.0, signs)
    got = 2.0 * packet_ref[0, total : total + 8, 0:lines].astype(jnp.float32) - 1.0
    got = jnp.where(first_part, 0.0, got)
    for l in range(lines):
        dirs[l, 0] = jnp.broadcast_to(signs[0:8, l : l + 1], (8, 128))
        dirs[l, 1] = jnp.broadcast_to(signs[8:16, l : l + 1], (8, 128))
        dirs[l, 2] = jnp.broadcast_to(got[0:1, l : l + 1], (8, 128))

    def side(t, carry):
        at = pl.ds(pl.multiple_of(t * 128, 128), 128)
        h0 = packet_ref[0, :, at].astype(jnp.float32)[0:total]
        h1 = packet_ref[1, :, at].astype(jnp.float32)[0:total]
        zero = jnp.zeros_like(h0)
        sides[0, t, 0:total] = jnp.where(first_part, zero, h1)
        sides[1, t, 0:total] = jnp.where(first_part, h0, zero)
        sides[2, t, 0:total] = jnp.where(first_part, h0 - 0.5 * (h1 - h0), h1 + 0.5 * (h1 - h0))
        sides[3, t, 0:total] = jnp.where(first_part, h1 - h0, zero)
        return carry

    lax.fori_loop(0, coeffs // 128, side, 0)
    row = lax.broadcasted_iota(jnp.int32, (8, 128), 0)
    top, bottom = row == 0, row == 7

    def down(low, high, edge):
        low_r, high_r = pltpu.roll(low, 1, 0), pltpu.roll(high, 1, 0)
        return jnp.where(top, edge, low_r), jnp.where(top, low_r, high_r)

    def up(low, high, edge):
        low_r, high_r = pltpu.roll(low, 7, 0), pltpu.roll(high, 7, 0)
        return jnp.where(bottom, high_r, low_r), jnp.where(bottom, edge, high_r)

    def one(l, carry):
        d0, d1, df = dirs[l, 0], dirs[l, 1], dirs[l, 2]
        p0, p1, pf = d0 > 0, d1 > 0, df > 0
        h0, h1 = jnp.where(p0, 0.5, -0.5), jnp.where(p1, 0.5, -0.5)
        for c in range(coeffs // 128):
            at = slice(c * 128, (c + 1) * 128)
            speed = courant * jnp.broadcast_to(speed_ref[:, at], (8, 128))
            v0, v1, vf = d0 * speed, d1 * speed, df * speed
            for s in range(species):
                f = cells_ref[s, l, :, at].astype(jnp.float32)
                f0, f1 = f[0:8], f[8:16]
                left, right, ext, diff = (
                    sides[k, c, pl.ds(s * lines + l, 8, stride=0), :] for k in range(4)
                )
                a0, a1 = up(f0, f1, right)
                b0, b1 = down(f0, f1, left)
                n0, n1 = a0 - f0, a1 - f1
                m0, m1 = up(n0, n1, diff)
                flux0 = v0 * (jnp.where(p0, f0, a0) + h0 * jnp.where(p0, f0 - b0, m0))
                flux1 = v1 * (jnp.where(p1, f1, a1) + h1 * jnp.where(p1, f1 - b1, m1))
                first = vf * jnp.where(pf, ext, f0 - 0.5 * n0)
                g0, g1 = down(flux0, flux1, first)
                new = jnp.concatenate([f0 - (flux0 - g0), f1 - (flux1 - g1)], axis=0)
                out_ref[s, l, :, at] = new.astype(jnp.bfloat16)
        return carry

    def part(c, carry):
        arriving(c).wait()
        lax.fori_loop(c * chunk, (c + 1) * chunk, one, 0)
        leaving(c).start()
        return carry

    lax.fori_loop(0, CHUNKS, part, 0)
    for c in range(CHUNKS):
        leaving(c).wait()


def transport(cells, packet, signs, speed, where):
    species, lines, _, coeffs = cells.shape
    return pl.pallas_call(
        transport_kernel,
        in_specs=[SMEM, VMEM, VMEM, VMEM, HBM],
        out_specs=[VMEM, HBM],
        out_shape=[
            pltpu.VMEM(cells.shape, jnp.bfloat16),
            jax.ShapeDtypeStruct(cells.shape, jnp.bfloat16),
        ],
        scratch_shapes=[
            pltpu.VMEM(cells.shape, jnp.bfloat16),
            pltpu.VMEM((4, coeffs // 128, species * lines + 8, 128), jnp.float32),
            pltpu.VMEM((cells.shape[1], 3, 8, 128), jnp.float32),
            DMA((CHUNKS,)),
            DMA((CHUNKS,)),
        ],
        cost_estimate=cost(30 * cells.size, 4 * cells.size),
        compiler_params=pltpu.CompilerParams(vmem_limit_bytes=16 << 20),
        name="transport",
    )(where, speed, signs, packet, stay(cells))


def join_kernel(*refs):
    out_ref = refs[-1]
    for i, ref in enumerate(refs[:-1]):
        out_ref[i] = ref[0]


def join(parts):
    shape = (len(parts),) + parts[0].shape[1:]
    return pl.pallas_call(
        join_kernel,
        in_specs=[VMEM] * len(parts),
        out_specs=VMEM,
        out_shape=pltpu.VMEM(shape, parts[0].dtype),
        cost_estimate=cost(parts[0].size, 16 * parts[0].size),
        compiler_params=pltpu.CompilerParams(vmem_limit_bytes=8 << 20),
        name="join",
    )(*parts)


def collide_kernel(units, first, last, freq_ref, pair_ref, adv_ref, *refs):
    count = sum(units)
    groups, refs = refs[:count], refs[count:]
    acc_ref, refs = (None, refs) if first else (refs[0], refs[1:])
    out_ref = refs[0]
    species, _, coeffs = adv_ref.shape
    pair_count = out_ref.shape[0]
    nt = (((1,), (1,)), ((), ()))
    ends = [sum(units[: k + 1]) for k in range(len(units))]
    held = [groups[end - n : end] for n, end in zip(units, ends)]

    def leaving(p):
        staged, out_sem = refs[1:]
        return pltpu.make_async_copy(staged.at[p], out_ref.at[p], out_sem.at[p])

    def ranks_of(arrays, which):
        return jnp.concatenate([ref[:, which].reshape(-1, coeffs) for ref in arrays], axis=0)

    left, right = [], []
    for s in range(species):
        both = [
            lax.dot_general(
                adv_ref[s],
                jnp.concatenate([ranks_of(h, 0), ranks_of(h, 1)], axis=0),
                nt,
                preferred_element_type=jnp.float32,
            )
            for h in held
        ]
        half = both[0].shape[1] // 2
        left.append(jnp.concatenate([b[:, :half] for b in both], axis=1))
        right.append(jnp.concatenate([b[:, half:] for b in both], axis=1))
    down = jnp.concatenate([ranks_of(h, 2) for h in held], axis=0)
    for p in range(pair_count):
        lp = jnp.where(pair_ref[0, p] == 1, left[1], left[0])
        rp = jnp.where(pair_ref[1, p] == 1, right[1], right[0])
        product = (freq_ref[p] * lp * rp).astype(jnp.bfloat16)
        term = jnp.dot(product, down, preferred_element_type=jnp.float32)
        if not first:
            term = (acc_ref if last else out_ref)[p] + term
        if last:
            refs[1][p] = term.astype(jnp.bfloat16)
            leaving(p).start()
        else:
            out_ref[p] = term
    if last:
        for p in range(pair_count):
            leaving(p).wait()


def collide(adv, frequency, pairs, held, acc, last=False):
    species, rows, coeffs = adv.shape
    pair_count = pairs.shape[1]
    groups = [array for unit in held for array in unit]
    ranks = sum(a.shape[0] * a.shape[2] for a in groups)
    shape = (pair_count, rows, coeffs)
    operands = [frequency, pairs, adv] + groups + ([] if acc is None else [acc])
    return pl.pallas_call(
        functools.partial(collide_kernel, [len(unit) for unit in held], acc is None, last),
        in_specs=[SMEM, SMEM] + [VMEM] * (len(operands) - 2),
        out_specs=HBM if last else VMEM,
        out_shape=jax.ShapeDtypeStruct(shape, jnp.bfloat16) if last else pltpu.VMEM(shape, jnp.float32),
        scratch_shapes=[pltpu.VMEM(shape, jnp.bfloat16), DMA((pair_count,))] if last else [],
        input_output_aliases={} if acc is None or last else {len(operands) - 1: 0},
        cost_estimate=cost(
            2 * ranks * coeffs * rows * (2 * species + pair_count),
            2 * (adv.size + 3 * ranks * coeffs),
        ),
        compiler_params=pltpu.CompilerParams(vmem_limit_bytes=20 << 20),
        name="collide",
    )(*operands)


def send(array, pairs):
    return lax.ppermute(array, AXES, pairs)


def phase(mine):
    return [mine, send(mine, UP1), send(mine, DOWN1)]


def relay(up, down):
    half = up.shape[0] // 2
    return [send(up[:half], UP2), send(down[half:], DOWN2)]


def swap(arrays):
    return [send(array, PARTNER) for array in arrays]


def after(array, *others):
    return lax.optimization_barrier((array,) + others)[0]


def local(distribution, face_signs, stream_speed, factors, pair_list, frequency):
    species, lines, cells, coeffs = distribution.shape
    here = lax.axis_index("space").astype(jnp.int32)[None]
    mine = factors[None]
    signs, pairs = face_signs.T, pair_list.T

    cross = send(mine, CROSS)
    parts_o = phase(mine) + [send(mine, FAR1)]
    parts_c = phase(cross) + [send(parts_o[3], CROSS)]
    packet = packet_of(distribution, signs, here)
    got = send(packet, SIDE)
    parts_o[0] = after(mine, packet)
    group_o = join(parts_o)
    up_o, down_o = send(group_o, UP2), send(group_o, DOWN2)
    swap_o = swap([group_o])
    adv_near, advanced = transport(distribution, got, signs, stream_speed[None], here)
    parts_c[0] = after(parts_c[0], adv_near)
    group_c = join(parts_c)
    up_c, down_c = send(group_c, UP2), send(group_c, DOWN2)
    swap_c = swap([group_c])

    adv = adv_near.reshape(species, lines * cells, coeffs)

    def step(held, acc, last=False):
        return collide(adv, frequency, pairs, held, acc, last)

    acc = step([[after(group_o, group_c)], swap_o], None)
    acc = step([[group_c], swap_c], acc)
    up_o, down_o, _ = lax.optimization_barrier((up_o, down_o, acc))
    far_o = relay(up_o, down_o)
    swap_uo, swap_do = swap([up_o]), swap([down_o])
    acc = step([[up_o], [down_o]], acc)
    acc = step([swap_uo, swap_do], acc)
    down_c, up_c, _ = lax.optimization_barrier((down_c, up_c, acc))
    far_c = relay(up_c, down_c)
    swap_dc, swap_uc = swap([down_c]), swap([up_c])
    acc = step([[down_c], [up_c]], acc)
    *far_o, _ = lax.optimization_barrier((*far_o, acc))
    swap_fo = swap(far_o)
    acc = step([swap_dc, swap_uc], acc)
    *far_c, _ = lax.optimization_barrier((*far_c, acc))
    swap_fc = swap(far_c)
    acc = step([far_o, swap_fo], acc)
    out = step([far_c, swap_fc], acc, last=True)
    collision = out.reshape(pair_list.shape[0], lines, cells, coeffs)
    return (advanced, collision)


def solution(mesh):
    return jax.shard_map(
        local,
        mesh=mesh,
        in_specs=(
            P(None, "blk", "space", None),
            P("blk", "space"),
            P(),
            P(None, "blk", None),
            P(),
            P(),
        ),
        out_specs=(P(None, "blk", "space", None), P(None, "blk", "space", None)),
        check_vma=False,
    )
```

```python
import functools
import jax
import jax.numpy as jnp
from jax import lax
from jax.experimental import pallas as pl
from jax.experimental.pallas import tpu as pltpu
from jax.sharding import PartitionSpec as P

courant = 0.3
AXES = ("blk", "space")
SIZES = (4, 4, 4, 2)


def flat_index(z, y, x, core):
    return (((z * 2 + y // 2) * 4 + x) * 2 + core) * 2 + y % 2


def pairs_of(move):
    pairs = []
    for z in range(4):
        for y in range(4):
            for x in range(4):
                for core in range(2):
                    target = [v % n for v, n in zip(move(z, y, x, core), SIZES)]
                    pairs.append((flat_index(z, y, x, core), flat_index(*target)))
    return pairs


def along(step, first):
    return pairs_of(
        lambda z, y, x, core: (z, y, x + step, core)
        if (core == 0) == first
        else (z + step, y, x, core)
    )


PARTNER = pairs_of(lambda z, y, x, core: (z, y, x, 1 - core))
CROSS = pairs_of(lambda z, y, x, core: (z, 3 - y, x, core))
SIDE = pairs_of(lambda z, y, x, core: (z, y ^ 1, x, core))
UP1, DOWN1, FAR1 = along(1, True), along(-1, True), along(2, True)
UP2, DOWN2 = along(1, False), along(-1, False)


SMEM = pl.BlockSpec(memory_space=pltpu.SMEM)
HBM = pl.BlockSpec(memory_space=pltpu.HBM)
VMEM = pl.BlockSpec(memory_space=pltpu.VMEM)
DMA = pltpu.SemaphoreType.DMA


def cost(flops, moved):
    return pl.CostEstimate(flops=flops, bytes_accessed=moved, transcendentals=0)


def stay(array):
    return pltpu.with_memory_space_constraint(array, pltpu.HBM)


def packet_kernel(where_ref, signs_hbm, cells_ref, out_ref, rows, edges, signs_ref, sem, sign_sem):
    first_part = where_ref[0] == 0
    species, lines, cells, coeffs = cells_ref.shape
    start = pl.multiple_of(jnp.where(first_part, cells - 8, 0), 8)
    copy = pltpu.make_async_copy(cells_ref.at[:, :, pl.ds(start, 8), :], rows, sem)
    copy.start()
    sign_copy = pltpu.make_async_copy(signs_hbm, signs_ref, sign_sem)
    sign_copy.start()
    total = species * lines
    edges[:, total:, :] = jnp.zeros((2, 8, coeffs), jnp.float32)
    sign_copy.wait()
    edges[0, total : total + 1, 0:lines] = signs_ref[cells - 1 : cells, :].astype(jnp.float32)
    copy.wait()

    def one(l, carry):
        for s in range(species):
            eight = rows[s, l].astype(jnp.float32)
            at = pl.ds(s * lines + l, 1)
            edges[0, at, :] = jnp.where(first_part, eight[6:7], eight[0:1])
            edges[1, at, :] = jnp.where(first_part, eight[7:8], eight[1:2])
        return carry

    lax.fori_loop(0, lines, one, 0)
    out_ref[...] = edges[...].astype(jnp.bfloat16)


def packet_of(cells, signs, where):
    species, lines, _, coeffs = cells.shape
    shape = (2, species * lines + 8, coeffs)
    return pl.pallas_call(
        packet_kernel,
        in_specs=[SMEM, HBM, HBM],
        out_specs=VMEM,
        out_shape=jax.ShapeDtypeStruct(shape, jnp.bfloat16),
        scratch_shapes=[
            pltpu.VMEM((species, lines, 8, coeffs), jnp.bfloat16),
            pltpu.VMEM(shape, jnp.float32),
            pltpu.VMEM(signs.shape, jnp.int32),
            DMA,
            DMA,
        ],
        cost_estimate=cost(cells.size, cells.size),
        compiler_params=pltpu.CompilerParams(vmem_limit_bytes=10 << 20),
        name="packet",
    )(where, stay(signs), stay(cells))


CHUNKS = 7


def transport_kernel(
    where_ref, speed_ref, signs_ref, packet_ref, cells_hbm, out_ref, out_hbm, cells_ref, sides, dirs, in_sem, out_sem
):
    first_part = where_ref[0] == 0
    species, lines, cells, coeffs = cells_ref.shape
    chunk = lines // CHUNKS
    total = species * lines

    def arriving(c):
        at = pl.ds(c * chunk, chunk)
        return pltpu.make_async_copy(cells_hbm.at[:, at], cells_ref.at[:, at], in_sem.at[c])

    def leaving(c):
        at = pl.ds(c * chunk, chunk)
        return pltpu.make_async_copy(out_ref.at[:, at], out_hbm.at[:, at], out_sem.at[c])

    for c in range(CHUNKS):
        arriving(c).start()

    column = lax.broadcasted_iota(jnp.int32, (cells, lines), 0)
    signs = (2 * signs_ref[...] - 1).astype(jnp.float32)
    signs = jnp.where(jnp.logical_and(column == cells - 1, jnp.logical_not(first_part)), 0.0, signs)
    got = 2.0 * packet_ref[0, total : total + 8, 0:lines].astype(jnp.float32) - 1.0
    got = jnp.where(first_part, 0.0, got)
    for l in range(lines):
        dirs[l, 0] = jnp.broadcast_to(signs[0:8, l : l + 1], (8, 128))
        dirs[l, 1] = jnp.broadcast_to(signs[8:16, l : l + 1], (8, 128))
        dirs[l, 2] = jnp.broadcast_to(got[0:1, l : l + 1], (8, 128))

    def side(t, carry):
        at = pl.ds(pl.multiple_of(t * 128, 128), 128)
        h0 = packet_ref[0, :, at].astype(jnp.float32)[0:total]
        h1 = packet_ref[1, :, at].astype(jnp.float32)[0:total]
        zero = jnp.zeros_like(h0)
        sides[0, t, 0:total] = jnp.where(first_part, zero, h1)
        sides[1, t, 0:total] = jnp.where(first_part, h0, zero)
        sides[2, t, 0:total] = jnp.where(first_part, h0 - 0.5 * (h1 - h0), h1 + 0.5 * (h1 - h0))
        sides[3, t, 0:total] = jnp.where(first_part, h1 - h0, zero)
        return carry

    lax.fori_loop(0, coeffs // 128, side, 0)
    row = lax.broadcasted_iota(jnp.int32, (8, 128), 0)
    top, bottom = row == 0, row == 7

    def down(low, high, edge):
        low_r, high_r = pltpu.roll(low, 1, 0), pltpu.roll(high, 1, 0)
        return jnp.where(top, edge, low_r), jnp.where(top, low_r, high_r)

    def up(low, high, edge):
        low_r, high_r = pltpu.roll(low, 7, 0), pltpu.roll(high, 7, 0)
        return jnp.where(bottom, high_r, low_r), jnp.where(bottom, edge, high_r)

    def one(l, carry):
        d0, d1, df = dirs[l, 0], dirs[l, 1], dirs[l, 2]
        p0, p1, pf = d0 > 0, d1 > 0, df > 0
        h0, h1 = jnp.where(p0, 0.5, -0.5), jnp.where(p1, 0.5, -0.5)
        for c in range(coeffs // 128):
            at = slice(c * 128, (c + 1) * 128)
            speed = courant * jnp.broadcast_to(speed_ref[:, at], (8, 128))
            v0, v1, vf = d0 * speed, d1 * speed, df * speed
            for s in range(species):
                f = cells_ref[s, l, :, at].astype(jnp.float32)
                f0, f1 = f[0:8], f[8:16]
                left, right, ext, diff = (
                    sides[k, c, pl.ds(s * lines + l, 8, stride=0), :] for k in range(4)
                )
                a0, a1 = up(f0, f1, right)
                b0, b1 = down(f0, f1, left)
                n0, n1 = a0 - f0, a1 - f1
                m0, m1 = up(n0, n1, diff)
                flux0 = v0 * (jnp.where(p0, f0, a0) + h0 * jnp.where(p0, f0 - b0, m0))
                flux1 = v1 * (jnp.where(p1, f1, a1) + h1 * jnp.where(p1, f1 - b1, m1))
                first = vf * jnp.where(pf, ext, f0 - 0.5 * n0)
                g0, g1 = down(flux0, flux1, first)
                new = jnp.concatenate([f0 - (flux0 - g0), f1 - (flux1 - g1)], axis=0)
                out_ref[s, l, :, at] = new.astype(jnp.bfloat16)
        return carry

    def part(c, carry):
        arriving(c).wait()
        lax.fori_loop(c * chunk, (c + 1) * chunk, one, 0)
        leaving(c).start()
        return carry

    lax.fori_loop(0, CHUNKS, part, 0)
    for c in range(CHUNKS):
        leaving(c).wait()


def transport(cells, packet, signs, speed, where):
    species, lines, _, coeffs = cells.shape
    return pl.pallas_call(
        transport_kernel,
        in_specs=[SMEM, VMEM, VMEM, VMEM, HBM],
        out_specs=[VMEM, HBM],
        out_shape=[
            pltpu.VMEM(cells.shape, jnp.bfloat16),
            jax.ShapeDtypeStruct(cells.shape, jnp.bfloat16),
        ],
        scratch_shapes=[
            pltpu.VMEM(cells.shape, jnp.bfloat16),
            pltpu.VMEM((4, coeffs // 128, species * lines + 8, 128), jnp.float32),
            pltpu.VMEM((cells.shape[1], 3, 8, 128), jnp.float32),
            DMA((CHUNKS,)),
            DMA((CHUNKS,)),
        ],
        cost_estimate=cost(30 * cells.size, 4 * cells.size),
        compiler_params=pltpu.CompilerParams(vmem_limit_bytes=16 << 20),
        name="transport",
    )(where, speed, signs, packet, stay(cells))


def join_kernel(*refs):
    out_ref = refs[-1]
    for i, ref in enumerate(refs[:-1]):
        out_ref[i] = ref[0]


def join(parts):
    shape = (len(parts),) + parts[0].shape[1:]
    return pl.pallas_call(
        join_kernel,
        in_specs=[VMEM] * len(parts),
        out_specs=VMEM,
        out_shape=pltpu.VMEM(shape, parts[0].dtype),
        cost_estimate=cost(parts[0].size, 16 * parts[0].size),
        compiler_params=pltpu.CompilerParams(vmem_limit_bytes=8 << 20),
        name="join",
    )(*parts)


def collide_kernel(units, first, last, freq_ref, pair_ref, adv_ref, *refs):
    count = sum(units)
    groups, refs = refs[:count], refs[count:]
    acc_ref, refs = (None, refs) if first else (refs[0], refs[1:])
    out_ref = refs[0]
    species, _, coeffs = adv_ref.shape
    pair_count = out_ref.shape[0]
    nt = (((1,), (1,)), ((), ()))
    ends = [sum(units[: k + 1]) for k in range(len(units))]
    held = [groups[end - n : end] for n, end in zip(units, ends)]

    width = coeffs // 2 if last else coeffs

    def leaving(p, c):
        staged, out_sem = refs[1:]
        at = pl.ds(c * width, width)
        return pltpu.make_async_copy(staged.at[p, :, at], out_ref.at[p, :, at], out_sem.at[p, c])

    def ranks_of(arrays, which):
        return jnp.concatenate([ref[:, which].reshape(-1, coeffs) for ref in arrays], axis=0)

    left, right = [], []
    for s in range(species):
        both = [
            lax.dot_general(
                adv_ref[s],
                jnp.concatenate([ranks_of(h, 0), ranks_of(h, 1)], axis=0),
                nt,
                preferred_element_type=jnp.float32,
            )
            for h in held
        ]
        half = both[0].shape[1] // 2
        left.append(jnp.concatenate([b[:, :half] for b in both], axis=1))
        right.append(jnp.concatenate([b[:, half:] for b in both], axis=1))
    down = jnp.concatenate([ranks_of(h, 2) for h in held], axis=0)
    for p in range(pair_count):
        lp = jnp.where(pair_ref[0, p] == 1, left[1], left[0])
        rp = jnp.where(pair_ref[1, p] == 1, right[1], right[0])
        product = (freq_ref[p] * lp * rp).astype(jnp.bfloat16)
        for c in range(coeffs // width):
            at = slice(c * width, (c + 1) * width)
            term = jnp.dot(product, down[:, at], preferred_element_type=jnp.float32)
            if not first:
                term = (acc_ref if last else out_ref)[p, :, at] + term
            if last:
                refs[1][p, :, at] = term.astype(jnp.bfloat16)
                leaving(p, c).start()
            else:
                out_ref[p, :, at] = term
    if last:
        for p in range(pair_count):
            for c in range(coeffs // width):
                leaving(p, c).wait()


def collide(adv, frequency, pairs, held, acc, last=False):
    species, rows, coeffs = adv.shape
    pair_count = pairs.shape[1]
    groups = [array for unit in held for array in unit]
    ranks = sum(a.shape[0] * a.shape[2] for a in groups)
    shape = (pair_count, rows, coeffs)
    operands = [frequency, pairs, adv] + groups + ([] if acc is None else [acc])
    return pl.pallas_call(
        functools.partial(collide_kernel, [len(unit) for unit in held], acc is None, last),
        in_specs=[SMEM, SMEM] + [VMEM] * (len(operands) - 2),
        out_specs=HBM if last else VMEM,
        out_shape=jax.ShapeDtypeStruct(shape, jnp.bfloat16) if last else pltpu.VMEM(shape, jnp.float32),
        scratch_shapes=[pltpu.VMEM(shape, jnp.bfloat16), DMA((pair_count, 2))] if last else [],
        input_output_aliases={} if acc is None or last else {len(operands) - 1: 0},
        cost_estimate=cost(
            2 * ranks * coeffs * rows * (2 * species + pair_count),
            2 * (adv.size + 3 * ranks * coeffs),
        ),
        compiler_params=pltpu.CompilerParams(vmem_limit_bytes=20 << 20),
        name="collide",
    )(*operands)


def send(array, pairs):
    return lax.ppermute(array, AXES, pairs)


def phase(mine):
    return [mine, send(mine, UP1), send(mine, DOWN1)]


def relay(up, down):
    half = up.shape[0] // 2
    return [send(up[:half], UP2), send(down[half:], DOWN2)]


def swap(arrays):
    return [send(array, PARTNER) for array in arrays]


def after(array, *others):
    return lax.optimization_barrier((array,) + others)[0]


def local(distribution, face_signs, stream_speed, factors, pair_list, frequency):
    species, lines, cells, coeffs = distribution.shape
    here = lax.axis_index("space").astype(jnp.int32)[None]
    mine = factors[None]
    signs, pairs = face_signs.T, pair_list.T

    cross = send(mine, CROSS)
    parts_o = phase(mine) + [send(mine, FAR1)]
    parts_c = phase(cross) + [send(parts_o[3], CROSS)]
    packet = packet_of(distribution, signs, here)
    got = send(packet, SIDE)
    parts_o[0] = after(mine, packet)
    group_o = join(parts_o)
    up_o, down_o = send(group_o, UP2), send(group_o, DOWN2)
    swap_o = swap([group_o])
    adv_near, advanced = transport(distribution, got, signs, stream_speed[None], here)
    parts_c[0] = after(parts_c[0], adv_near)
    group_c = join(parts_c)
    up_c, down_c = send(group_c, UP2), send(group_c, DOWN2)
    swap_c = swap([group_c])

    adv = adv_near.reshape(species, lines * cells, coeffs)

    def step(held, acc, last=False):
        return collide(adv, frequency, pairs, held, acc, last)

    acc = step([[after(group_o, group_c)], swap_o], None)
    acc = step([[group_c], swap_c], acc)
    up_o, down_o, _ = lax.optimization_barrier((up_o, down_o, acc))
    far_o = relay(up_o, down_o)
    swap_uo, swap_do = swap([up_o]), swap([down_o])
    acc = step([[up_o], [down_o]], acc)
    acc = step([swap_uo, swap_do], acc)
    down_c, up_c, _ = lax.optimization_barrier((down_c, up_c, acc))
    far_c = relay(up_c, down_c)
    swap_dc, swap_uc = swap([down_c]), swap([up_c])
    acc = step([[down_c], [up_c]], acc)
    *far_o, _ = lax.optimization_barrier((*far_o, acc))
    swap_fo = swap(far_o)
    acc = step([swap_dc, swap_uc], acc)
    acc = step([far_o, swap_fo], acc)
    *far_c, _ = lax.optimization_barrier((*far_c, acc))
    swap_fc = swap(far_c)
    out = step([far_c, swap_fc], acc, last=True)
    collision = out.reshape(pair_list.shape[0], lines, cells, coeffs)
    return (advanced, collision)


def solution(mesh):
    return jax.shard_map(
        local,
        mesh=mesh,
        in_specs=(
            P(None, "blk", "space", None),
            P("blk", "space"),
            P(),
            P(None, "blk", None),
            P(),
            P(),
        ),
        out_specs=(P(None, "blk", "space", None), P(None, "blk", "space", None)),
        check_vma=False,
    )
```

```python
import functools
import jax
import jax.numpy as jnp
from jax import lax
from jax.experimental import pallas as pl
from jax.experimental.pallas import tpu as pltpu
from jax.sharding import PartitionSpec as P

courant = 0.3
AXES = ("blk", "space")
SIZES = (4, 4, 4, 2)


def flat_index(z, y, x, core):
    return (((z * 2 + y // 2) * 4 + x) * 2 + core) * 2 + y % 2


def pairs_of(move):
    pairs = []
    for z in range(4):
        for y in range(4):
            for x in range(4):
                for core in range(2):
                    target = [v % n for v, n in zip(move(z, y, x, core), SIZES)]
                    pairs.append((flat_index(z, y, x, core), flat_index(*target)))
    return pairs


def along(step, first):
    return pairs_of(
        lambda z, y, x, core: (z, y, x + step, core)
        if (core == 0) == first
        else (z + step, y, x, core)
    )


PARTNER = pairs_of(lambda z, y, x, core: (z, y, x, 1 - core))
CROSS = pairs_of(lambda z, y, x, core: (z, 3 - y, x, core))
SIDE = pairs_of(lambda z, y, x, core: (z, y ^ 1, x, core))
UP1, DOWN1, FAR1 = along(1, True), along(-1, True), along(2, True)
UP2, DOWN2 = along(1, False), along(-1, False)


SMEM = pl.BlockSpec(memory_space=pltpu.SMEM)
HBM = pl.BlockSpec(memory_space=pltpu.HBM)
VMEM = pl.BlockSpec(memory_space=pltpu.VMEM)
DMA = pltpu.SemaphoreType.DMA


def cost(flops, moved):
    return pl.CostEstimate(flops=flops, bytes_accessed=moved, transcendentals=0)


def stay(array):
    return pltpu.with_memory_space_constraint(array, pltpu.HBM)


def packet_kernel(where_ref, signs_hbm, cells_ref, out_ref, rows, edges, signs_ref, sem, sign_sem):
    first_part = where_ref[0] == 0
    species, lines, cells, coeffs = cells_ref.shape
    start = pl.multiple_of(jnp.where(first_part, cells - 8, 0), 8)
    copy = pltpu.make_async_copy(cells_ref.at[:, :, pl.ds(start, 8), :], rows, sem)
    copy.start()
    sign_copy = pltpu.make_async_copy(signs_hbm, signs_ref, sign_sem)
    sign_copy.start()
    total = species * lines
    edges[:, total:, :] = jnp.zeros((2, 8, coeffs), jnp.float32)
    sign_copy.wait()
    edges[0, total : total + 1, 0:lines] = signs_ref[cells - 1 : cells, :].astype(jnp.float32)
    copy.wait()

    def one(l, carry):
        for s in range(species):
            eight = rows[s, l].astype(jnp.float32)
            at = pl.ds(s * lines + l, 1)
            edges[0, at, :] = jnp.where(first_part, eight[6:7], eight[0:1])
            edges[1, at, :] = jnp.where(first_part, eight[7:8], eight[1:2])
        return carry

    lax.fori_loop(0, lines, one, 0)
    out_ref[...] = edges[...].astype(jnp.bfloat16)


def packet_of(cells, signs, where):
    species, lines, _, coeffs = cells.shape
    shape = (2, species * lines + 8, coeffs)
    return pl.pallas_call(
        packet_kernel,
        in_specs=[SMEM, HBM, HBM],
        out_specs=VMEM,
        out_shape=jax.ShapeDtypeStruct(shape, jnp.bfloat16),
        scratch_shapes=[
            pltpu.VMEM((species, lines, 8, coeffs), jnp.bfloat16),
            pltpu.VMEM(shape, jnp.float32),
            pltpu.VMEM(signs.shape, jnp.int32),
            DMA,
            DMA,
        ],
        cost_estimate=cost(cells.size, cells.size),
        compiler_params=pltpu.CompilerParams(vmem_limit_bytes=10 << 20),
        name="packet",
    )(where, stay(signs), stay(cells))


CHUNKS = 7


def face_signs_of(signs_ref):
    return (2 * signs_ref[...] - 1).astype(jnp.float32)


def rows_iota():
    return lax.broadcasted_iota(jnp.int32, (8, 128), 0)


def low_half(f0, f1, face, left, first):
    v, p, h = face
    row = rows_iota()
    low, high = pltpu.roll(f0, 7, 0), pltpu.roll(f1, 7, 0)
    a = jnp.where(row == 7, high, low)
    n = a - f0
    m = jnp.where(row == 7, pltpu.roll(high - f1, 7, 0), pltpu.roll(n, 7, 0))
    b = jnp.where(row == 0, left, pltpu.roll(f0, 1, 0))
    flux = v * (jnp.where(p, f0, a) + h * jnp.where(p, f0 - b, m))
    before = jnp.where(row == 0, first(n), pltpu.roll(flux, 1, 0))
    return f0 - (flux - before)


def high_half(f0, f1, face, right, last):
    v, p, h = face
    row = rows_iota()
    b = jnp.where(row == 0, pltpu.roll(f0, 1, 0), pltpu.roll(f1, 1, 0))
    bb = jnp.where(row < 2, pltpu.roll(f0, 2, 0), pltpu.roll(f1, 2, 0))
    a = jnp.where(row == 7, right, pltpu.roll(f1, 7, 0))
    flux = v * (jnp.where(p, b, f1) + h * jnp.where(p, b - bb, a - f1))
    behind = jnp.where(row == 7, last(b), pltpu.roll(flux, 7, 0))
    return f1 - (behind - flux)


def over_lines(start, stop, cells_ref, speed_ref, dirs, new_half, low, out_ref):
    species, _, _, coeffs = cells_ref.shape

    def one(l, carry):
        d = dirs[l]
        p = d > 0
        h = jnp.where(p, 0.5, -0.5)
        for c in range(coeffs // 128):
            at = slice(c * 128, (c + 1) * 128)
            speed = courant * jnp.broadcast_to(speed_ref[:, at], (8, 128))
            face = (d * speed, p, h)
            for s in range(species):
                f = cells_ref[s, l, :, at].astype(jnp.float32)
                new = new_half(f[0:8], f[8:16], face, s, l, c, speed)
                rows = slice(0, 8) if low else slice(8, 16)
                out_ref[s, l, rows, at] = new.astype(jnp.bfloat16)
        return carry

    lax.fori_loop(start, stop, one, 0)


def wall_kernel(where_ref, speed_ref, signs_ref, cells_hbm, cells_ref, out_ref, dirs, in_sem):
    first_part = where_ref[0] == 0
    _, lines, _, _ = cells_ref.shape
    chunk = lines // CHUNKS

    def arriving(c):
        at = pl.ds(c * chunk, chunk)
        return pltpu.make_async_copy(cells_hbm.at[:, at], cells_ref.at[:, at], in_sem.at[c])

    for c in range(CHUNKS):
        arriving(c).start()
    signs = face_signs_of(signs_ref)
    base = jnp.where(first_part, signs[0:8], signs[7:15])
    for l in range(lines):
        dirs[l] = jnp.broadcast_to(base[:, l : l + 1], (8, 128))

    def low(f0, f1, face, s, l, c, speed):
        return low_half(f0, f1, face, 0.0, lambda n: 0.0)

    def high(f0, f1, face, s, l, c, speed):
        return high_half(f0, f1, face, 0.0, lambda b: 0.0)

    def part(c, carry):
        arriving(c).wait()

        @pl.when(first_part)
        def _():
            over_lines(c * chunk, (c + 1) * chunk, cells_ref, speed_ref, dirs, low, True, out_ref)

        @pl.when(jnp.logical_not(first_part))
        def _():
            over_lines(c * chunk, (c + 1) * chunk, cells_ref, speed_ref, dirs, high, False, out_ref)

        return carry

    lax.fori_loop(0, CHUNKS, part, 0)


def halo_kernel(
    where_ref, speed_ref, signs_ref, packet_ref, cells_ref, wall_ref, out_ref, out_hbm, sides, dirs, ends, out_sem
):
    first_part = where_ref[0] == 0
    species, lines, _, coeffs = cells_ref.shape
    chunk = lines // CHUNKS
    total = species * lines

    def leaving(c):
        at = pl.ds(c * chunk, chunk)
        return pltpu.make_async_copy(out_ref.at[:, at], out_hbm.at[:, at], out_sem.at[c])

    signs = face_signs_of(signs_ref)
    got = 2.0 * packet_ref[0, total : total + 8, 0:lines].astype(jnp.float32) - 1.0
    base = jnp.where(first_part, signs[7:15], signs[0:8])
    end = jnp.where(first_part, signs[15:16], got[0:1])
    for l in range(lines):
        dirs[l] = jnp.broadcast_to(base[:, l : l + 1], (8, 128))
        ends[l] = jnp.broadcast_to(end[:, l : l + 1], (8, 128))

    def side(t, carry):
        at = pl.ds(pl.multiple_of(t * 128, 128), 128)
        h0 = packet_ref[0, :, at].astype(jnp.float32)[0:total]
        h1 = packet_ref[1, :, at].astype(jnp.float32)[0:total]
        sides[0, t, 0:total] = jnp.where(first_part, h0, h1)
        sides[1, t, 0:total] = jnp.where(first_part, h1 - h0, h1 + 0.5 * (h1 - h0))
        return carry

    lax.fori_loop(0, coeffs // 128, side, 0)

    def beyond(k, s, l, c):
        return sides[k, c, pl.ds(s * lines + l, 8, stride=0), :]

    def low(f0, f1, face, s, l, c, speed):
        d = ends[l]

        def first(n):
            return d * speed * jnp.where(d > 0, beyond(1, s, l, c), f0 - 0.5 * n)

        return low_half(f0, f1, face, beyond(0, s, l, c), first)

    def high(f0, f1, face, s, l, c, speed):
        d = ends[l]
        right = beyond(0, s, l, c)

        def last(b):
            h = jnp.where(d > 0, 0.5, -0.5)
            return d * speed * (jnp.where(d > 0, f1, right) + h * jnp.where(d > 0, f1 - b, beyond(1, s, l, c)))

        return high_half(f0, f1, face, right, last)

    def part(c, carry):
        @pl.when(first_part)
        def _():
            over_lines(c * chunk, (c + 1) * chunk, cells_ref, speed_ref, dirs, high, False, out_ref)

        @pl.when(jnp.logical_not(first_part))
        def _():
            over_lines(c * chunk, (c + 1) * chunk, cells_ref, speed_ref, dirs, low, True, out_ref)

        leaving(c).start()
        return carry

    lax.fori_loop(0, CHUNKS, part, 0)
    for c in range(CHUNKS):
        leaving(c).wait()


def wall_half(cells, signs, speed, where):
    lines = cells.shape[1]
    return pl.pallas_call(
        wall_kernel,
        in_specs=[SMEM, VMEM, VMEM, HBM],
        out_specs=[VMEM, VMEM],
        out_shape=[pltpu.VMEM(cells.shape, jnp.bfloat16)] * 2,
        scratch_shapes=[pltpu.VMEM((lines, 8, 128), jnp.float32), DMA((CHUNKS,))],
        cost_estimate=cost(15 * cells.size, 4 * cells.size),
        compiler_params=pltpu.CompilerParams(vmem_limit_bytes=8 << 20),
        name="wall_half",
    )(where, speed, signs, stay(cells))


def halo_half(cells, wall, packet, signs, speed, where):
    species, lines, _, coeffs = cells.shape
    return pl.pallas_call(
        halo_kernel,
        in_specs=[SMEM] + [VMEM] * 5,
        out_specs=[VMEM, HBM],
        out_shape=[
            pltpu.VMEM(cells.shape, jnp.bfloat16),
            jax.ShapeDtypeStruct(cells.shape, jnp.bfloat16),
        ],
        scratch_shapes=[
            pltpu.VMEM((2, coeffs // 128, species * lines + 8, 128), jnp.float32),
            pltpu.VMEM((lines, 8, 128), jnp.float32),
            pltpu.VMEM((lines, 8, 128), jnp.float32),
            DMA((CHUNKS,)),
        ],
        input_output_aliases={5: 0},
        cost_estimate=cost(20 * cells.size, 4 * cells.size),
        compiler_params=pltpu.CompilerParams(vmem_limit_bytes=10 << 20),
        name="halo_half",
    )(where, speed, signs, packet, cells, wall)


def join_kernel(*refs):
    out_ref = refs[-1]
    for i, ref in enumerate(refs[:-1]):
        out_ref[i] = ref[0]


def join(parts):
    shape = (len(parts),) + parts[0].shape[1:]
    return pl.pallas_call(
        join_kernel,
        in_specs=[VMEM] * len(parts),
        out_specs=VMEM,
        out_shape=pltpu.VMEM(shape, parts[0].dtype),
        cost_estimate=cost(parts[0].size, 16 * parts[0].size),
        compiler_params=pltpu.CompilerParams(vmem_limit_bytes=8 << 20),
        name="join",
    )(*parts)


def collide_kernel(units, first, last, freq_ref, pair_ref, adv_ref, *refs):
    count = sum(units)
    groups, refs = refs[:count], refs[count:]
    acc_ref, refs = (None, refs) if first else (refs[0], refs[1:])
    out_ref = refs[0]
    species, _, coeffs = adv_ref.shape
    pair_count = out_ref.shape[0]
    nt = (((1,), (1,)), ((), ()))
    ends = [sum(units[: k + 1]) for k in range(len(units))]
    held = [groups[end - n : end] for n, end in zip(units, ends)]

    width = coeffs // 2 if last else coeffs

    def leaving(p, c):
        staged, out_sem = refs[1:]
        at = pl.ds(c * width, width)
        return pltpu.make_async_copy(staged.at[p, :, at], out_ref.at[p, :, at], out_sem.at[p, c])

    def ranks_of(arrays, which):
        return jnp.concatenate([ref[:, which].reshape(-1, coeffs) for ref in arrays], axis=0)

    left, right = [], []
    for s in range(species):
        both = [
            lax.dot_general(
                adv_ref[s],
                jnp.concatenate([ranks_of(h, 0), ranks_of(h, 1)], axis=0),
                nt,
                preferred_element_type=jnp.float32,
            )
            for h in held
        ]
        half = both[0].shape[1] // 2
        left.append(jnp.concatenate([b[:, :half] for b in both], axis=1))
        right.append(jnp.concatenate([b[:, half:] for b in both], axis=1))
    down = jnp.concatenate([ranks_of(h, 2) for h in held], axis=0)
    for p in range(pair_count):
        lp = jnp.where(pair_ref[0, p] == 1, left[1], left[0])
        rp = jnp.where(pair_ref[1, p] == 1, right[1], right[0])
        product = (freq_ref[p] * lp * rp).astype(jnp.bfloat16)
        for c in range(coeffs // width):
            at = slice(c * width, (c + 1) * width)
            term = jnp.dot(product, down[:, at], preferred_element_type=jnp.float32)
            if not first:
                term = (acc_ref if last else out_ref)[p, :, at] + term
            if last:
                refs[1][p, :, at] = term.astype(jnp.bfloat16)
                leaving(p, c).start()
            else:
                out_ref[p, :, at] = term
    if last:
        for p in range(pair_count):
            for c in range(coeffs // width):
                leaving(p, c).wait()


def collide(adv, frequency, pairs, held, acc, last=False):
    species, rows, coeffs = adv.shape
    pair_count = pairs.shape[1]
    groups = [array for unit in held for array in unit]
    ranks = sum(a.shape[0] * a.shape[2] for a in groups)
    shape = (pair_count, rows, coeffs)
    operands = [frequency, pairs, adv] + groups + ([] if acc is None else [acc])
    return pl.pallas_call(
        functools.partial(collide_kernel, [len(unit) for unit in held], acc is None, last),
        in_specs=[SMEM, SMEM] + [VMEM] * (len(operands) - 2),
        out_specs=HBM if last else VMEM,
        out_shape=jax.ShapeDtypeStruct(shape, jnp.bfloat16) if last else pltpu.VMEM(shape, jnp.float32),
        scratch_shapes=[pltpu.VMEM(shape, jnp.bfloat16), DMA((pair_count, 2))] if last else [],
        input_output_aliases={} if acc is None or last else {len(operands) - 1: 0},
        cost_estimate=cost(
            2 * ranks * coeffs * rows * (2 * species + pair_count),
            2 * (adv.size + 3 * ranks * coeffs),
        ),
        compiler_params=pltpu.CompilerParams(vmem_limit_bytes=20 << 20),
        name="collide",
    )(*operands)


def send(array, pairs):
    return lax.ppermute(array, AXES, pairs)


def phase(mine):
    return [mine, send(mine, UP1), send(mine, DOWN1)]


def relay(up, down):
    half = up.shape[0] // 2
    return [send(up[:half], UP2), send(down[half:], DOWN2)]


def swap(arrays):
    return [send(array, PARTNER) for array in arrays]


def after(array, *others):
    return lax.optimization_barrier((array,) + others)[0]


def local(distribution, face_signs, stream_speed, factors, pair_list, frequency):
    species, lines, cells, coeffs = distribution.shape
    here = lax.axis_index("space").astype(jnp.int32)[None]
    mine = factors[None]
    signs, pairs = face_signs.T, pair_list.T

    cross = send(mine, CROSS)
    parts_o = phase(mine) + [send(mine, FAR1)]
    parts_c = phase(cross) + [send(parts_o[3], CROSS)]
    packet = packet_of(distribution, signs, here)
    got = send(packet, SIDE)
    near, wall = wall_half(distribution, signs, stream_speed[None], here)
    parts_o[0] = after(mine, packet, wall)
    group_o = join(parts_o)
    up_o, down_o = send(group_o, UP2), send(group_o, DOWN2)
    swap_o = swap([group_o])
    adv_near, advanced = halo_half(near, wall, got, signs, stream_speed[None], here)
    parts_c[0] = after(parts_c[0], adv_near)
    group_c = join(parts_c)
    up_c, down_c = send(group_c, UP2), send(group_c, DOWN2)
    swap_c = swap([group_c])

    adv = adv_near.reshape(species, lines * cells, coeffs)

    def step(held, acc, last=False):
        return collide(adv, frequency, pairs, held, acc, last)

    acc = step([[after(group_o, group_c)], swap_o], None)
    acc = step([[group_c], swap_c], acc)
    up_o, down_o, _ = lax.optimization_barrier((up_o, down_o, acc))
    far_o = relay(up_o, down_o)
    swap_uo, swap_do = swap([up_o]), swap([down_o])
    acc = step([[up_o], [down_o]], acc)
    acc = step([swap_uo, swap_do], acc)
    down_c, up_c, _ = lax.optimization_barrier((down_c, up_c, acc))
    far_c = relay(up_c, down_c)
    swap_dc, swap_uc = swap([down_c]), swap([up_c])
    acc = step([[down_c], [up_c]], acc)
    *far_o, _ = lax.optimization_barrier((*far_o, acc))
    swap_fo = swap(far_o)
    acc = step([swap_dc, swap_uc], acc)
    acc = step([far_o, swap_fo], acc)
    *far_c, _ = lax.optimization_barrier((*far_c, acc))
    swap_fc = swap(far_c)
    out = step([far_c, swap_fc], acc, last=True)
    collision = out.reshape(pair_list.shape[0], lines, cells, coeffs)
    return (advanced, collision)


def solution(mesh):
    return jax.shard_map(
        local,
        mesh=mesh,
        in_specs=(
            P(None, "blk", "space", None),
            P("blk", "space"),
            P(),
            P(None, "blk", None),
            P(),
            P(),
        ),
        out_specs=(P(None, "blk", "space", None), P(None, "blk", "space", None)),
        check_vma=False,
    )
```

```python
import functools
import jax
import jax.numpy as jnp
from jax import lax
from jax.experimental import pallas as pl
from jax.experimental.pallas import tpu as pltpu
from jax.sharding import PartitionSpec as P

courant = 0.3
AXES = ("blk", "space")
SIZES = (4, 4, 4, 2)


def flat_index(z, y, x, core):
    return (((z * 2 + y // 2) * 4 + x) * 2 + core) * 2 + y % 2


def pairs_of(move):
    pairs = []
    for z in range(4):
        for y in range(4):
            for x in range(4):
                for core in range(2):
                    target = [v % n for v, n in zip(move(z, y, x, core), SIZES)]
                    pairs.append((flat_index(z, y, x, core), flat_index(*target)))
    return pairs


def along(step, first):
    return pairs_of(
        lambda z, y, x, core: (z, y, x + step, core)
        if (core == 0) == first
        else (z + step, y, x, core)
    )


PARTNER = pairs_of(lambda z, y, x, core: (z, y, x, 1 - core))
CROSS = pairs_of(lambda z, y, x, core: (z, 3 - y, x, core))
SIDE = pairs_of(lambda z, y, x, core: (z, y ^ 1, x, core))
UP1, DOWN1, FAR1 = along(1, True), along(-1, True), along(2, True)
UP2, DOWN2 = along(1, False), along(-1, False)


SMEM = pl.BlockSpec(memory_space=pltpu.SMEM)
HBM = pl.BlockSpec(memory_space=pltpu.HBM)
VMEM = pl.BlockSpec(memory_space=pltpu.VMEM)
DMA = pltpu.SemaphoreType.DMA


def cost(flops, moved):
    return pl.CostEstimate(flops=flops, bytes_accessed=moved, transcendentals=0)


def stay(array):
    return pltpu.with_memory_space_constraint(array, pltpu.HBM)


def packet_kernel(where_ref, signs_hbm, cells_ref, out_ref, rows, edges, signs_ref, sem, sign_sem):
    first_part = where_ref[0] == 0
    species, lines, cells, coeffs = cells_ref.shape
    start = pl.multiple_of(jnp.where(first_part, cells - 8, 0), 8)
    copy = pltpu.make_async_copy(cells_ref.at[:, :, pl.ds(start, 8), :], rows, sem)
    copy.start()
    sign_copy = pltpu.make_async_copy(signs_hbm, signs_ref, sign_sem)
    sign_copy.start()
    total = species * lines
    edges[:, total:, :] = jnp.zeros((2, 8, coeffs), jnp.float32)
    sign_copy.wait()
    edges[0, total : total + 1, 0:lines] = signs_ref[cells - 1 : cells, :].astype(jnp.float32)
    copy.wait()

    def one(l, carry):
        for s in range(species):
            eight = rows[s, l].astype(jnp.float32)
            at = pl.ds(s * lines + l, 1)
            edges[0, at, :] = jnp.where(first_part, eight[6:7], eight[0:1])
            edges[1, at, :] = jnp.where(first_part, eight[7:8], eight[1:2])
        return carry

    lax.fori_loop(0, lines, one, 0)

    def rounded(c, carry):
        at = pl.ds(pl.multiple_of(c * 256, 256), 256)
        out_ref[:, :, at] = edges[:, :, at].astype(jnp.bfloat16)
        return carry

    lax.fori_loop(0, coeffs // 256, rounded, 0)


def packet_of(cells, signs, where):
    species, lines, _, coeffs = cells.shape
    shape = (2, species * lines + 8, coeffs)
    return pl.pallas_call(
        packet_kernel,
        in_specs=[SMEM, HBM, HBM],
        out_specs=VMEM,
        out_shape=jax.ShapeDtypeStruct(shape, jnp.bfloat16),
        scratch_shapes=[
            pltpu.VMEM((species, lines, 8, coeffs), jnp.bfloat16),
            pltpu.VMEM(shape, jnp.float32),
            pltpu.VMEM(signs.shape, jnp.int32),
            DMA,
            DMA,
        ],
        cost_estimate=cost(cells.size, cells.size),
        compiler_params=pltpu.CompilerParams(vmem_limit_bytes=10 << 20),
        name="packet",
    )(where, stay(signs), stay(cells))


CHUNKS = 7


def transport_kernel(
    where_ref, speed_ref, signs_ref, packet_ref, cells_hbm, out_ref, out_hbm, cells_ref, sides, dirs, in_sem, out_sem
):
    first_part = where_ref[0] == 0
    species, lines, cells, coeffs = cells_ref.shape
    chunk = lines // CHUNKS
    total = species * lines

    def arriving(c):
        at = pl.ds(c * chunk, chunk)
        return pltpu.make_async_copy(cells_hbm.at[:, at], cells_ref.at[:, at], in_sem.at[c])

    def leaving(c):
        at = pl.ds(c * chunk, chunk)
        return pltpu.make_async_copy(out_ref.at[:, at], out_hbm.at[:, at], out_sem.at[c])

    for c in range(CHUNKS):
        arriving(c).start()

    column = lax.broadcasted_iota(jnp.int32, (cells, lines), 0)
    signs = (2 * signs_ref[...] - 1).astype(jnp.float32)
    signs = jnp.where(jnp.logical_and(column == cells - 1, jnp.logical_not(first_part)), 0.0, signs)
    got = 2.0 * packet_ref[0, total : total + 8, 0:lines].astype(jnp.float32) - 1.0
    got = jnp.where(first_part, 0.0, got)
    for l in range(lines):
        dirs[l, 0] = jnp.broadcast_to(signs[0:8, l : l + 1], (8, 128))
        dirs[l, 1] = jnp.broadcast_to(signs[8:16, l : l + 1], (8, 128))
        dirs[l, 2] = jnp.broadcast_to(got[0:1, l : l + 1], (8, 128))

    def side(t, carry):
        at = pl.ds(pl.multiple_of(t * 128, 128), 128)
        h0 = packet_ref[0, :, at].astype(jnp.float32)[0:total]
        h1 = packet_ref[1, :, at].astype(jnp.float32)[0:total]
        zero = jnp.zeros_like(h0)
        sides[0, t, 0:total] = jnp.where(first_part, zero, h1)
        sides[1, t, 0:total] = jnp.where(first_part, h0, zero)
        sides[2, t, 0:total] = jnp.where(first_part, h0 - 0.5 * (h1 - h0), h1 + 0.5 * (h1 - h0))
        sides[3, t, 0:total] = jnp.where(first_part, h1 - h0, zero)
        return carry

    lax.fori_loop(0, coeffs // 128, side, 0)
    row = lax.broadcasted_iota(jnp.int32, (8, 128), 0)
    top, bottom = row == 0, row == 7

    def down(low, high, edge):
        low_r, high_r = pltpu.roll(low, 1, 0), pltpu.roll(high, 1, 0)
        return jnp.where(top, edge, low_r), jnp.where(top, low_r, high_r)

    def up(low, high, edge):
        low_r, high_r = pltpu.roll(low, 7, 0), pltpu.roll(high, 7, 0)
        return jnp.where(bottom, high_r, low_r), jnp.where(bottom, edge, high_r)

    def one(l, carry):
        d0, d1, df = dirs[l, 0], dirs[l, 1], dirs[l, 2]
        p0, p1, pf = d0 > 0, d1 > 0, df > 0
        h0, h1 = jnp.where(p0, 0.5, -0.5), jnp.where(p1, 0.5, -0.5)

        def some(q, carry):
            for k in range(8):
                c = q * 8 + k
                at = pl.ds(pl.multiple_of(c * 128, 128), 128)
                speed = courant * jnp.broadcast_to(speed_ref[:, at], (8, 128))
                v0, v1, vf = d0 * speed, d1 * speed, df * speed
                for s in range(species):
                    f = cells_ref[s, l, :, at].astype(jnp.float32)
                    f0, f1 = f[0:8], f[8:16]
                    left, right, ext, diff = (
                        sides[k, c, pl.ds(s * lines + l, 8, stride=0), :] for k in range(4)
                    )
                    a0, a1 = up(f0, f1, right)
                    b0, b1 = down(f0, f1, left)
                    n0, n1 = a0 - f0, a1 - f1
                    m0, m1 = up(n0, n1, diff)
                    flux0 = v0 * (jnp.where(p0, f0, a0) + h0 * jnp.where(p0, f0 - b0, m0))
                    flux1 = v1 * (jnp.where(p1, f1, a1) + h1 * jnp.where(p1, f1 - b1, m1))
                    first = vf * jnp.where(pf, ext, f0 - 0.5 * n0)
                    g0, g1 = down(flux0, flux1, first)
                    new = jnp.concatenate([f0 - (flux0 - g0), f1 - (flux1 - g1)], axis=0)
                    out_ref[s, l, :, at] = new.astype(jnp.bfloat16)
            return carry

        lax.fori_loop(0, coeffs // 1024, some, 0)
        return carry

    def part(c, carry):
        arriving(c).wait()
        lax.fori_loop(c * chunk, (c + 1) * chunk, one, 0)
        leaving(c).start()
        return carry

    lax.fori_loop(0, CHUNKS, part, 0)
    for c in range(CHUNKS):
        leaving(c).wait()


def transport(cells, packet, signs, speed, where):
    species, lines, _, coeffs = cells.shape
    return pl.pallas_call(
        transport_kernel,
        in_specs=[SMEM, VMEM, VMEM, VMEM, HBM],
        out_specs=[VMEM, HBM],
        out_shape=[
            pltpu.VMEM(cells.shape, jnp.bfloat16),
            jax.ShapeDtypeStruct(cells.shape, jnp.bfloat16),
        ],
        scratch_shapes=[
            pltpu.VMEM(cells.shape, jnp.bfloat16),
            pltpu.VMEM((4, coeffs // 128, species * lines + 8, 128), jnp.float32),
            pltpu.VMEM((cells.shape[1], 3, 8, 128), jnp.float32),
            DMA((CHUNKS,)),
            DMA((CHUNKS,)),
        ],
        cost_estimate=cost(30 * cells.size, 4 * cells.size),
        compiler_params=pltpu.CompilerParams(vmem_limit_bytes=16 << 20),
        name="transport",
    )(where, speed, signs, packet, stay(cells))


def join_kernel(*refs):
    out_ref = refs[-1]
    for i, ref in enumerate(refs[:-1]):
        out_ref[i] = ref[0]


def join(parts):
    shape = (len(parts),) + parts[0].shape[1:]
    return pl.pallas_call(
        join_kernel,
        in_specs=[VMEM] * len(parts),
        out_specs=VMEM,
        out_shape=pltpu.VMEM(shape, parts[0].dtype),
        cost_estimate=cost(parts[0].size, 16 * parts[0].size),
        compiler_params=pltpu.CompilerParams(vmem_limit_bytes=8 << 20),
        name="join",
    )(*parts)


def collide_kernel(units, first, last, freq_ref, pair_ref, adv_ref, *refs):
    count = sum(units)
    groups, refs = refs[:count], refs[count:]
    acc_ref, refs = (None, refs) if first else (refs[0], refs[1:])
    out_ref = refs[0]
    species, rows, coeffs = adv_ref.shape
    pair_count = out_ref.shape[0]
    nt = (((1,), (1,)), ((), ()))
    ends = [sum(units[: k + 1]) for k in range(len(units))]
    held = [groups[end - n : end] for n, end in zip(units, ends)]

    blocks = 2 if last else 1
    block = rows // blocks

    def leaving(p, i):
        staged, out_sem = refs[1:]
        at = pl.ds(pl.multiple_of(i * block, block), block)
        return pltpu.make_async_copy(staged.at[p, at], out_ref.at[p, at], out_sem.at[p, i])

    def ranks_of(arrays, which):
        return jnp.concatenate([ref[:, which].reshape(-1, coeffs) for ref in arrays], axis=0)

    def one(i, carry):
        at = pl.ds(pl.multiple_of(i * block, block), block)
        left, right = [], []
        for s in range(species):
            both = [
                lax.dot_general(
                    adv_ref[s, at, :],
                    jnp.concatenate([ranks_of(h, 0), ranks_of(h, 1)], axis=0),
                    nt,
                    preferred_element_type=jnp.float32,
                )
                for h in held
            ]
            half = both[0].shape[1] // 2
            left.append(jnp.concatenate([b[:, :half] for b in both], axis=1))
            right.append(jnp.concatenate([b[:, half:] for b in both], axis=1))
        down = jnp.concatenate([ranks_of(h, 2) for h in held], axis=0)
        for p in range(pair_count):
            lp = jnp.where(pair_ref[0, p] == 1, left[1], left[0])
            rp = jnp.where(pair_ref[1, p] == 1, right[1], right[0])
            product = (freq_ref[p] * lp * rp).astype(jnp.bfloat16)
            term = jnp.dot(product, down, preferred_element_type=jnp.float32)
            if not first:
                term = (acc_ref if last else out_ref)[p, at, :] + term
            if last:
                refs[1][p, at, :] = term.astype(jnp.bfloat16)
                leaving(p, i).start()
            else:
                out_ref[p, at, :] = term
        return carry

    if not last:
        one(0, 0)
        return
    lax.fori_loop(0, blocks, one, 0)
    for p in range(pair_count):
        for i in range(blocks):
            leaving(p, i).wait()


def collide(adv, frequency, pairs, held, acc, last=False):
    species, rows, coeffs = adv.shape
    pair_count = pairs.shape[1]
    groups = [array for unit in held for array in unit]
    ranks = sum(a.shape[0] * a.shape[2] for a in groups)
    shape = (pair_count, rows, coeffs)
    operands = [frequency, pairs, adv] + groups + ([] if acc is None else [acc])
    return pl.pallas_call(
        functools.partial(collide_kernel, [len(unit) for unit in held], acc is None, last),
        in_specs=[SMEM, SMEM] + [VMEM] * (len(operands) - 2),
        out_specs=HBM if last else VMEM,
        out_shape=jax.ShapeDtypeStruct(shape, jnp.bfloat16) if last else pltpu.VMEM(shape, jnp.float32),
        scratch_shapes=[pltpu.VMEM(shape, jnp.bfloat16), DMA((pair_count, 2))] if last else [],
        input_output_aliases={} if acc is None or last else {len(operands) - 1: 0},
        cost_estimate=cost(
            2 * ranks * coeffs * rows * (2 * species + pair_count),
            2 * (adv.size + 3 * ranks * coeffs),
        ),
        compiler_params=pltpu.CompilerParams(vmem_limit_bytes=20 << 20),
        name="collide",
    )(*operands)


def send(array, pairs):
    return lax.ppermute(array, AXES, pairs)


def phase(mine):
    return [mine, send(mine, UP1), send(mine, DOWN1)]


def relay(up, down):
    half = up.shape[0] // 2
    return [send(up[:half], UP2), send(down[half:], DOWN2)]


def swap(arrays):
    return [send(array, PARTNER) for array in arrays]


def after(array, *others):
    return lax.optimization_barrier((array,) + others)[0]


def local(distribution, face_signs, stream_speed, factors, pair_list, frequency):
    species, lines, cells, coeffs = distribution.shape
    here = lax.axis_index("space").astype(jnp.int32)[None]
    mine = factors[None]
    signs, pairs = face_signs.T, pair_list.T

    cross = send(mine, CROSS)
    parts_o = phase(mine) + [send(mine, FAR1)]
    parts_c = phase(cross) + [send(parts_o[3], CROSS)]
    packet = packet_of(distribution, signs, here)
    got = send(packet, SIDE)
    up_m, down_m = send(mine, UP2), send(mine, DOWN2)
    parts_o[1] = after(parts_o[1], packet)
    rest_o = join(parts_o[1:])
    up_r, down_r = send(rest_o, UP2), send(rest_o, DOWN2)
    group_o = [mine, rest_o]
    swap_o = swap(group_o)
    adv_near, advanced = transport(distribution, got, signs, stream_speed[None], here)
    parts_c[0] = after(parts_c[0], adv_near)
    group_c = join(parts_c)
    up_c, down_c = send(group_c, UP2), send(group_c, DOWN2)
    swap_c = swap([group_c])

    adv = adv_near.reshape(species, lines * cells, coeffs)

    def step(held, acc, last=False):
        return collide(adv, frequency, pairs, held, acc, last)

    rest_o = after(rest_o, group_c)
    acc = step([[mine, rest_o], swap_o], None)
    acc = step([[group_c], swap_c], acc)
    up_r, down_r, _ = lax.optimization_barrier((up_r, down_r, acc))
    far_o = [send(up_r[:2], UP2), send(jnp.concatenate([down_m, down_r[2:]], axis=0), DOWN2)]
    up_o, down_o = [up_m, up_r], [down_m, down_r]
    swap_uo, swap_do = swap(up_o), swap(down_o)
    acc = step([up_o, down_o], acc)
    acc = step([swap_uo, swap_do], acc)
    down_c, up_c, _ = lax.optimization_barrier((down_c, up_c, acc))
    far_c = relay(up_c, down_c)
    swap_dc, swap_uc = swap([down_c]), swap([up_c])
    acc = step([[down_c], [up_c]], acc)
    *far_o, _ = lax.optimization_barrier((*far_o, acc))
    swap_fo = swap(far_o)
    acc = step([swap_dc, swap_uc], acc)
    *far_c, _ = lax.optimization_barrier((*far_c, acc))
    swap_fc = swap(far_c)
    acc = step([far_o, swap_fo], acc)
    out = step([far_c, swap_fc], acc, last=True)
    collision = out.reshape(pair_list.shape[0], lines, cells, coeffs)
    return (advanced, collision)


def solution(mesh):
    return jax.shard_map(
        local,
        mesh=mesh,
        in_specs=(
            P(None, "blk", "space", None),
            P("blk", "space"),
            P(),
            P(None, "blk", None),
            P(),
            P(),
        ),
        out_specs=(P(None, "blk", "space", None), P(None, "blk", "space", None)),
        check_vma=False,
    )
```

```python
import functools
import jax
import jax.numpy as jnp
from jax import lax
from jax.experimental import pallas as pl
from jax.experimental.pallas import tpu as pltpu
from jax.sharding import PartitionSpec as P

courant = 0.3
AXES = ("blk", "space")
SIZES = (4, 4, 4, 2)


def flat_index(z, y, x, core):
    return (((z * 2 + y // 2) * 4 + x) * 2 + core) * 2 + y % 2


def pairs_of(move):
    pairs = []
    for z in range(4):
        for y in range(4):
            for x in range(4):
                for core in range(2):
                    target = [v % n for v, n in zip(move(z, y, x, core), SIZES)]
                    pairs.append((flat_index(z, y, x, core), flat_index(*target)))
    return pairs


def along(step, first):
    return pairs_of(
        lambda z, y, x, core: (z, y, x + step, core)
        if (core == 0) == first
        else (z + step, y, x, core)
    )


PARTNER = pairs_of(lambda z, y, x, core: (z, y, x, 1 - core))
CROSS = pairs_of(lambda z, y, x, core: (z, 3 - y, x, core))
SIDE = pairs_of(lambda z, y, x, core: (z, y ^ 1, x, core))
UP1, DOWN1, FAR1 = along(1, True), along(-1, True), along(2, True)
UP2, DOWN2 = along(1, False), along(-1, False)


SMEM = pl.BlockSpec(memory_space=pltpu.SMEM)
HBM = pl.BlockSpec(memory_space=pltpu.HBM)
VMEM = pl.BlockSpec(memory_space=pltpu.VMEM)
DMA = pltpu.SemaphoreType.DMA


def cost(flops, moved):
    return pl.CostEstimate(flops=flops, bytes_accessed=moved, transcendentals=0)


def stay(array):
    return pltpu.with_memory_space_constraint(array, pltpu.HBM)


def packet_kernel(where_ref, signs_hbm, cells_ref, out_ref, rows, edges, signs_ref, sem, sign_sem):
    first_part = where_ref[0] == 0
    species, lines, cells, coeffs = cells_ref.shape
    start = pl.multiple_of(jnp.where(first_part, cells - 8, 0), 8)
    copy = pltpu.make_async_copy(cells_ref.at[:, :, pl.ds(start, 8), :], rows, sem)
    copy.start()
    sign_copy = pltpu.make_async_copy(signs_hbm, signs_ref, sign_sem)
    sign_copy.start()
    total = species * lines
    edges[:, total:, :] = jnp.zeros((2, 8, coeffs), jnp.float32)
    sign_copy.wait()
    edges[0, total : total + 1, 0:lines] = signs_ref[cells - 1 : cells, :].astype(jnp.float32)
    copy.wait()

    def one(l, carry):
        for s in range(species):
            eight = rows[s, l].astype(jnp.float32)
            at = pl.ds(s * lines + l, 1)
            edges[0, at, :] = jnp.where(first_part, eight[6:7], eight[0:1])
            edges[1, at, :] = jnp.where(first_part, eight[7:8], eight[1:2])
        return carry

    lax.fori_loop(0, lines, one, 0)

    def rounded(c, carry):
        at = pl.ds(pl.multiple_of(c * 256, 256), 256)
        out_ref[:, :, at] = edges[:, :, at].astype(jnp.bfloat16)
        return carry

    lax.fori_loop(0, coeffs // 256, rounded, 0)


def packet_of(cells, signs, where):
    species, lines, _, coeffs = cells.shape
    shape = (2, species * lines + 8, coeffs)
    return pl.pallas_call(
        packet_kernel,
        in_specs=[SMEM, HBM, HBM],
        out_specs=VMEM,
        out_shape=jax.ShapeDtypeStruct(shape, jnp.bfloat16),
        scratch_shapes=[
            pltpu.VMEM((species, lines, 8, coeffs), jnp.bfloat16),
            pltpu.VMEM(shape, jnp.float32),
            pltpu.VMEM(signs.shape, jnp.int32),
            DMA,
            DMA,
        ],
        cost_estimate=cost(cells.size, cells.size),
        compiler_params=pltpu.CompilerParams(vmem_limit_bytes=10 << 20),
        name="packet",
    )(where, stay(signs), stay(cells))


CHUNKS = 7


def face_signs_of(signs_ref):
    return (2 * signs_ref[...] - 1).astype(jnp.float32)


def rows_iota():
    return lax.broadcasted_iota(jnp.int32, (8, 128), 0)


def low_half(f0, f1, face, left, first):
    v, p, h = face
    row = rows_iota()
    low, high = pltpu.roll(f0, 7, 0), pltpu.roll(f1, 7, 0)
    a = jnp.where(row == 7, high, low)
    n = a - f0
    m = jnp.where(row == 7, pltpu.roll(high - f1, 7, 0), pltpu.roll(n, 7, 0))
    b = jnp.where(row == 0, left, pltpu.roll(f0, 1, 0))
    flux = v * (jnp.where(p, f0, a) + h * jnp.where(p, f0 - b, m))
    before = jnp.where(row == 0, first(n), pltpu.roll(flux, 1, 0))
    return f0 - (flux - before)


def high_half(f0, f1, face, right, last):
    v, p, h = face
    row = rows_iota()
    b = jnp.where(row == 0, pltpu.roll(f0, 1, 0), pltpu.roll(f1, 1, 0))
    bb = jnp.where(row < 2, pltpu.roll(f0, 2, 0), pltpu.roll(f1, 2, 0))
    a = jnp.where(row == 7, right, pltpu.roll(f1, 7, 0))
    flux = v * (jnp.where(p, b, f1) + h * jnp.where(p, b - bb, a - f1))
    behind = jnp.where(row == 7, last(b), pltpu.roll(flux, 7, 0))
    return f1 - (behind - flux)


def over_lines(start, stop, cells_ref, speed_ref, dirs, new_half, low, out_ref):
    species, _, _, coeffs = cells_ref.shape

    def one(l, carry):
        d = dirs[l]
        p = d > 0
        h = jnp.where(p, 0.5, -0.5)
        rows = slice(0, 8) if low else slice(8, 16)

        def some(q, carry):
            for k in range(8):
                c = q * 8 + k
                at = pl.ds(pl.multiple_of(c * 128, 128), 128)
                speed = courant * jnp.broadcast_to(speed_ref[:, at], (8, 128))
                face = (d * speed, p, h)
                for s in range(species):
                    f = cells_ref[s, l, :, at].astype(jnp.float32)
                    new = new_half(f[0:8], f[8:16], face, s, l, c, speed)
                    out_ref[s, l, rows, at] = new.astype(jnp.bfloat16)
            return carry

        return lax.fori_loop(0, coeffs // 1024, some, carry)

    lax.fori_loop(start, stop, one, 0)


def wall_kernel(where_ref, speed_ref, signs_ref, cells_hbm, cells_ref, out_ref, dirs, in_sem):
    first_part = where_ref[0] == 0
    _, lines, _, _ = cells_ref.shape
    chunk = lines // CHUNKS

    def arriving(c):
        at = pl.ds(c * chunk, chunk)
        return pltpu.make_async_copy(cells_hbm.at[:, at], cells_ref.at[:, at], in_sem.at[c])

    for c in range(CHUNKS):
        arriving(c).start()
    signs = face_signs_of(signs_ref)
    base = jnp.where(first_part, signs[0:8], signs[7:15])
    for l in range(lines):
        dirs[l] = jnp.broadcast_to(base[:, l : l + 1], (8, 128))

    def low(f0, f1, face, s, l, c, speed):
        return low_half(f0, f1, face, 0.0, lambda n: 0.0)

    def high(f0, f1, face, s, l, c, speed):
        return high_half(f0, f1, face, 0.0, lambda b: 0.0)

    def part(c, carry):
        arriving(c).wait()

        @pl.when(first_part)
        def _():
            over_lines(c * chunk, (c + 1) * chunk, cells_ref, speed_ref, dirs, low, True, out_ref)

        @pl.when(jnp.logical_not(first_part))
        def _():
            over_lines(c * chunk, (c + 1) * chunk, cells_ref, speed_ref, dirs, high, False, out_ref)

        return carry

    lax.fori_loop(0, CHUNKS, part, 0)


def halo_kernel(
    where_ref, speed_ref, signs_ref, packet_ref, cells_ref, wall_ref, out_ref, out_hbm, sides, dirs, ends, out_sem
):
    first_part = where_ref[0] == 0
    species, lines, _, coeffs = cells_ref.shape
    chunk = lines // CHUNKS
    total = species * lines

    def leaving(c):
        at = pl.ds(c * chunk, chunk)
        return pltpu.make_async_copy(out_ref.at[:, at], out_hbm.at[:, at], out_sem.at[c])

    signs = face_signs_of(signs_ref)
    got = 2.0 * packet_ref[0, total : total + 8, 0:lines].astype(jnp.float32) - 1.0
    base = jnp.where(first_part, signs[7:15], signs[0:8])
    end = jnp.where(first_part, signs[15:16], got[0:1])
    for l in range(lines):
        dirs[l] = jnp.broadcast_to(base[:, l : l + 1], (8, 128))
        ends[l] = jnp.broadcast_to(end[:, l : l + 1], (8, 128))

    def side(t, carry):
        at = pl.ds(pl.multiple_of(t * 128, 128), 128)
        h0 = packet_ref[0, :, at].astype(jnp.float32)[0:total]
        h1 = packet_ref[1, :, at].astype(jnp.float32)[0:total]
        sides[0, t, 0:total] = jnp.where(first_part, h0, h1)
        sides[1, t, 0:total] = jnp.where(first_part, h1 - h0, h1 + 0.5 * (h1 - h0))
        return carry

    lax.fori_loop(0, coeffs // 128, side, 0)

    def beyond(k, s, l, c):
        return sides[k, c, pl.ds(s * lines + l, 8, stride=0), :]

    def low(f0, f1, face, s, l, c, speed):
        d = ends[l]

        def first(n):
            return d * speed * jnp.where(d > 0, beyond(1, s, l, c), f0 - 0.5 * n)

        return low_half(f0, f1, face, beyond(0, s, l, c), first)

    def high(f0, f1, face, s, l, c, speed):
        d = ends[l]
        right = beyond(0, s, l, c)

        def last(b):
            h = jnp.where(d > 0, 0.5, -0.5)
            return d * speed * (jnp.where(d > 0, f1, right) + h * jnp.where(d > 0, f1 - b, beyond(1, s, l, c)))

        return high_half(f0, f1, face, right, last)

    def part(c, carry):
        @pl.when(first_part)
        def _():
            over_lines(c * chunk, (c + 1) * chunk, cells_ref, speed_ref, dirs, high, False, out_ref)

        @pl.when(jnp.logical_not(first_part))
        def _():
            over_lines(c * chunk, (c + 1) * chunk, cells_ref, speed_ref, dirs, low, True, out_ref)

        leaving(c).start()
        return carry

    lax.fori_loop(0, CHUNKS, part, 0)
    for c in range(CHUNKS):
        leaving(c).wait()


def wall_half(cells, signs, speed, where):
    lines = cells.shape[1]
    return pl.pallas_call(
        wall_kernel,
        in_specs=[SMEM, VMEM, VMEM, HBM],
        out_specs=[VMEM, VMEM],
        out_shape=[pltpu.VMEM(cells.shape, jnp.bfloat16)] * 2,
        scratch_shapes=[pltpu.VMEM((lines, 8, 128), jnp.float32), DMA((CHUNKS,))],
        cost_estimate=cost(15 * cells.size, 4 * cells.size),
        compiler_params=pltpu.CompilerParams(vmem_limit_bytes=8 << 20),
        name="wall_half",
    )(where, speed, signs, stay(cells))


def halo_half(cells, wall, packet, signs, speed, where):
    species, lines, _, coeffs = cells.shape
    return pl.pallas_call(
        halo_kernel,
        in_specs=[SMEM] + [VMEM] * 5,
        out_specs=[VMEM, HBM],
        out_shape=[
            pltpu.VMEM(cells.shape, jnp.bfloat16),
            jax.ShapeDtypeStruct(cells.shape, jnp.bfloat16),
        ],
        scratch_shapes=[
            pltpu.VMEM((2, coeffs // 128, species * lines + 8, 128), jnp.float32),
            pltpu.VMEM((lines, 8, 128), jnp.float32),
            pltpu.VMEM((lines, 8, 128), jnp.float32),
            DMA((CHUNKS,)),
        ],
        input_output_aliases={5: 0},
        cost_estimate=cost(20 * cells.size, 4 * cells.size),
        compiler_params=pltpu.CompilerParams(vmem_limit_bytes=10 << 20),
        name="halo_half",
    )(where, speed, signs, packet, cells, wall)


def join_kernel(*refs):
    out_ref = refs[-1]
    for i, ref in enumerate(refs[:-1]):
        out_ref[i] = ref[0]


def join(parts):
    shape = (len(parts),) + parts[0].shape[1:]
    return pl.pallas_call(
        join_kernel,
        in_specs=[VMEM] * len(parts),
        out_specs=VMEM,
        out_shape=pltpu.VMEM(shape, parts[0].dtype),
        cost_estimate=cost(parts[0].size, 16 * parts[0].size),
        compiler_params=pltpu.CompilerParams(vmem_limit_bytes=8 << 20),
        name="join",
    )(*parts)


def collide_kernel(units, first, last, freq_ref, pair_ref, adv_ref, *refs):
    count = sum(units)
    groups, refs = refs[:count], refs[count:]
    acc_ref, refs = (None, refs) if first else (refs[0], refs[1:])
    out_ref = refs[0]
    species, _, coeffs = adv_ref.shape
    pair_count = out_ref.shape[0]
    nt = (((1,), (1,)), ((), ()))
    ends = [sum(units[: k + 1]) for k in range(len(units))]
    held = [groups[end - n : end] for n, end in zip(units, ends)]

    width = coeffs // 2 if last else coeffs

    def leaving(p, c):
        staged, out_sem = refs[1:]
        at = pl.ds(c * width, width)
        return pltpu.make_async_copy(staged.at[p, :, at], out_ref.at[p, :, at], out_sem.at[p, c])

    def ranks_of(arrays, which):
        return jnp.concatenate([ref[:, which].reshape(-1, coeffs) for ref in arrays], axis=0)

    left, right = [], []
    for s in range(species):
        both = [
            lax.dot_general(
                adv_ref[s],
                jnp.concatenate([ranks_of(h, 0), ranks_of(h, 1)], axis=0),
                nt,
                preferred_element_type=jnp.float32,
            )
            for h in held
        ]
        half = both[0].shape[1] // 2
        left.append(jnp.concatenate([b[:, :half] for b in both], axis=1))
        right.append(jnp.concatenate([b[:, half:] for b in both], axis=1))
    down = jnp.concatenate([ranks_of(h, 2) for h in held], axis=0)
    for p in range(pair_count):
        lp = jnp.where(pair_ref[0, p] == 1, left[1], left[0])
        rp = jnp.where(pair_ref[1, p] == 1, right[1], right[0])
        product = (freq_ref[p] * lp * rp).astype(jnp.bfloat16)
        for c in range(coeffs // width):
            at = slice(c * width, (c + 1) * width)
            term = jnp.dot(product, down[:, at], preferred_element_type=jnp.float32)
            if not first:
                term = (acc_ref if last else out_ref)[p, :, at] + term
            if last:
                refs[1][p, :, at] = term.astype(jnp.bfloat16)
                leaving(p, c).start()
            else:
                out_ref[p, :, at] = term
    if last:
        for p in range(pair_count):
            for c in range(coeffs // width):
                leaving(p, c).wait()


def collide(adv, frequency, pairs, held, acc, last=False):
    species, rows, coeffs = adv.shape
    pair_count = pairs.shape[1]
    groups = [array for unit in held for array in unit]
    ranks = sum(a.shape[0] * a.shape[2] for a in groups)
    shape = (pair_count, rows, coeffs)
    operands = [frequency, pairs, adv] + groups + ([] if acc is None else [acc])
    return pl.pallas_call(
        functools.partial(collide_kernel, [len(unit) for unit in held], acc is None, last),
        in_specs=[SMEM, SMEM] + [VMEM] * (len(operands) - 2),
        out_specs=HBM if last else VMEM,
        out_shape=jax.ShapeDtypeStruct(shape, jnp.bfloat16) if last else pltpu.VMEM(shape, jnp.float32),
        scratch_shapes=[pltpu.VMEM(shape, jnp.bfloat16), DMA((pair_count, 2))] if last else [],
        input_output_aliases={} if acc is None or last else {len(operands) - 1: 0},
        cost_estimate=cost(
            2 * ranks * coeffs * rows * (2 * species + pair_count),
            2 * (adv.size + 3 * ranks * coeffs),
        ),
        compiler_params=pltpu.CompilerParams(vmem_limit_bytes=20 << 20),
        name="collide",
    )(*operands)


def send(array, pairs):
    return lax.ppermute(array, AXES, pairs)


def phase(mine):
    return [mine, send(mine, UP1), send(mine, DOWN1)]


def relay(up, down):
    half = up.shape[0] // 2
    return [send(up[:half], UP2), send(down[half:], DOWN2)]


def swap(arrays):
    return [send(array, PARTNER) for array in arrays]


def after(array, *others):
    return lax.optimization_barrier((array,) + others)[0]


def local(distribution, face_signs, stream_speed, factors, pair_list, frequency):
    species, lines, cells, coeffs = distribution.shape
    here = lax.axis_index("space").astype(jnp.int32)[None]
    mine = factors[None]
    signs, pairs = face_signs.T, pair_list.T

    cross = send(mine, CROSS)
    parts_o = phase(mine) + [send(mine, FAR1)]
    parts_c = phase(cross) + [send(parts_o[3], CROSS)]
    packet = packet_of(distribution, signs, here)
    got = send(packet, SIDE)
    near, wall = wall_half(distribution, signs, stream_speed[None], here)
    parts_o[0] = after(mine, packet, wall)
    group_o = join(parts_o)
    up_o, down_o = send(group_o, UP2), send(group_o, DOWN2)
    swap_o = swap([group_o])
    adv_near, advanced = halo_half(near, wall, got, signs, stream_speed[None], here)
    parts_c[0] = after(parts_c[0], adv_near)
    group_c = join(parts_c)
    up_c, down_c = send(group_c, UP2), send(group_c, DOWN2)
    swap_c = swap([group_c])

    adv = adv_near.reshape(species, lines * cells, coeffs)

    def step(held, acc, last=False):
        return collide(adv, frequency, pairs, held, acc, last)

    acc = step([[after(group_o, group_c)], swap_o], None)
    acc = step([[group_c], swap_c], acc)
    up_o, down_o, _ = lax.optimization_barrier((up_o, down_o, acc))
    far_o = relay(up_o, down_o)
    swap_uo, swap_do = swap([up_o]), swap([down_o])
    acc = step([[up_o], [down_o]], acc)
    acc = step([swap_uo, swap_do], acc)
    down_c, up_c, _ = lax.optimization_barrier((down_c, up_c, acc))
    far_c = relay(up_c, down_c)
    swap_dc, swap_uc = swap([down_c]), swap([up_c])
    acc = step([[down_c], [up_c]], acc)
    *far_o, _ = lax.optimization_barrier((*far_o, acc))
    swap_fo = swap(far_o)
    acc = step([swap_dc, swap_uc], acc)
    acc = step([far_o, swap_fo], acc)
    *far_c, _ = lax.optimization_barrier((*far_c, acc))
    swap_fc = swap(far_c)
    out = step([far_c, swap_fc], acc, last=True)
    collision = out.reshape(pair_list.shape[0], lines, cells, coeffs)
    return (advanced, collision)


def solution(mesh):
    return jax.shard_map(
        local,
        mesh=mesh,
        in_specs=(
            P(None, "blk", "space", None),
            P("blk", "space"),
            P(),
            P(None, "blk", None),
            P(),
            P(),
        ),
        out_specs=(P(None, "blk", "space", None), P(None, "blk", "space", None)),
        check_vma=False,
    )
```
